128 devices in a mesh: member: 4 (over y), space: 32 (over z, x, core).
Axes of the slice: x: 4, y: 4, z: 4, core: 2. Of those that a mesh axis runs over, the one named last changes fastest.
Arguments:
- grid_in: bfloat16 [4, 32768, 256], P('member', 'space'), may hold values from -6 to 6
- mesh_embed: bfloat16 [8192, 512], P('space'), may hold values from -6 to 6
- g2m_src: int32 [32, 32, 256], P('space'), may hold values from 0 to 1023
- g2m_dst: int32 [32, 32, 256], P('space'), may hold values from 0 to 255
- g2m_own_src: int32 [32, 1536], P('space'), may hold values from 0 to 1023
- g2m_own_dst: int32 [32, 1536], P('space'), may hold values from 0 to 255
- g2m_len: int32 [32, 32], P(None, 'space'), may hold values from 0 to 1536, as said below
- mesh_nbr: int32 [8192, 32], P('space'), may hold values from 0 to 767
- halo_rows: int32 [32, 16], P('space'), may hold values from 0 to 255
- m2g_src: int32 [32, 32, 256], P('space'), may hold values from 0 to 255
- m2g_dst: int32 [32, 32, 256], P('space'), may hold values from 0 to 1023
- m2g_own_src: int32 [32, 2560], P('space'), may hold values from 0 to 255
- m2g_own_dst: int32 [32, 2560], P('space'), may hold values from 0 to 1023
- m2g_len: int32 [32, 32], P(None, 'space'), may hold values from 0 to 2560, as said below
- w_embed: bfloat16 [256, 512], replicated, may hold values from -0.375 to 0.375
- w_send: bfloat16 [512, 512], replicated, may hold values from -0.25 to 0.25
- w_mesh: bfloat16 [512, 512], replicated, may hold values from -0.25 to 0.25
- attn_gain: float32 [512], replicated, may hold values from 0.1 to 1.9
- w_query: bfloat16 [512, 512], P('member')
- w_key: bfloat16 [512, 512], P('member')
- w_value: bfloat16 [512, 512], P('member'), may hold values from -0.25 to 0.25
- w_project: bfloat16 [512, 512], P('member'), may hold values from -0.25 to 0.25
- mlp_gain: float32 [512], replicated, may hold values from 0.1 to 1.9
- w_up: bfloat16 [512, 2048], P('member'), may hold values from -0.25 to 0.25
- w_down: bfloat16 [2048, 512], P('member'), may hold values from -0.125 to 0.125
- w_return: bfloat16 [512, 512], replicated, may hold values from -0.25 to 0.25
- w_grid: bfloat16 [512, 512], replicated, may hold values from -0.25 to 0.25
- w_skip: bfloat16 [512, 512], replicated, may hold values from -0.25 to 0.25
- w_out: bfloat16 [512, 84], replicated, may hold values from -0.25 to 0.25
Outputs:
- denoised: bfloat16 [4, 84, 32768], P('member', None, 'space')
The draws below stay inside these ranges and needn't reach their ends.
Inputs may be any that keep to these rules, and one draw needn't show every extreme that they name: Pairs with |s - d| > 1 are empty (length 0). For |s - d| = 1 slot j carries an edge exactly when j < g2m_len[s, d] <= 256; on the diagonal, slot j of g2m_own_src and g2m_own_dst carries an edge exactly when j < g2m_len[p, p] <= 1536. Other slots hold arbitrary indices. The bands at the two ends of the axis (4 at each) receive the most edges. Pairs with |s - d| > 1 are empty (length 0). For |s - d| = 1 slot j carries an edge exactly when j < m2g_len[s, d] <= 256; on the diagonal, slot j of m2g_own_src and m2g_own_dst carries an edge exactly when j < m2g_len[p, p] <= 2560. Other slots hold arbitrary indices. The bands at the two ends of the axis (4 at each) receive the most edges.
All inputs are finite; a program needn't handle non-finite values.
Results may differ from the reference program's by a relative error of at most 0.015.
Values may be sent and summed in bfloat16 or wider, within the bound.
No kernel may reach another device: no remote copies, remote signals or barrier semaphores. Data moves between devices by JAX's collectives and lax.ppermute only.
A program may use at most 64 MiB of HBM per device.

```python
import math
import jax
import jax.numpy as jnp
from jax import lax

D = 512
F_IN = 256
F_OUT = 84
H = 4
DH = 128
FFN = 2048
K_NBR = 32
G_DEV = 1024
M_DEV = 256
SLOTS = 256
G2M_OWN = 1536
M2G_OWN = 2560
HB = 16
BANDS = 32
MEMBERS = 4
GRID = 32768
MESH = 8192


def pair_lengths(key, own_capacity):
    sender = lax.broadcasted_iota(jnp.int32, (BANDS, BANDS), 0)
    target = lax.broadcasted_iota(jnp.int32, (BANDS, BANDS), 1)
    heavy = (target < BANDS // 8) | (target >= BANDS - BANDS // 8)
    spread = jax.random.randint(key, (BANDS, BANDS), 0, 1 << 20)
    diagonal = jnp.where(heavy, own_capacity, own_capacity // 2 + spread % (own_capacity // 4 + 1))
    nearby = jnp.where(heavy, SLOTS, SLOTS // 4 + spread % (SLOTS // 4 + 1))
    apart = jnp.abs(sender - target)
    return jnp.where(apart == 0, diagonal, jnp.where(apart == 1, nearby, 0)).astype(jnp.int32)


def draw_g2m_len(key, part):
    return pair_lengths(jax.random.fold_in(key, 11), G2M_OWN)


def draw_m2g_len(key, part):
    return pair_lengths(jax.random.fold_in(key, 12), M2G_OWN)


def draw_mesh_nbr(key, part):
    first = jax.random.fold_in(key, 21)
    second = jax.random.fold_in(key, 22)
    third = jax.random.fold_in(key, 23)
    shape = (MESH, K_NBR)
    picker = jax.random.randint(first, shape, 0, 4)
    local_pick = jax.random.randint(second, shape, 0, M_DEV)
    remote_pick = M_DEV + jax.random.randint(third, shape, 0, BANDS * HB)
    return jnp.where(picker == 0, remote_pick, local_pick).astype(jnp.int32)


def head_weight(key, which):
    own_part = jax.random.normal(jax.random.fold_in(key, 32 + which), (D, D), jnp.float32)
    mixed = own_part / jnp.sqrt(jnp.float32(D))
    return mixed.astype(jnp.bfloat16)


def draw_w_query(key, part):
    return head_weight(key, 1)


def draw_w_key(key, part):
    return head_weight(key, 2)


def plant(drawn, stream_key, low, largest):
    spot = [jax.random.randint(jax.random.fold_in(stream_key, axis), (), 0, length) for axis, length in enumerate(drawn.shape)]
    widest = drawn.shape.index(max(drawn.shape))
    next_to = spot[:widest] + [(spot[widest] + 1) % drawn.shape[widest]] + spot[widest + 1:]
    return drawn.at[tuple(spot)].set(low).at[tuple(next_to)].set(largest)


def levels(rng, dims, shards, least, top_value):
    def one(position, parts):
        heights = jax.random.uniform(jax.random.fold_in(jax.random.fold_in(rng, 6), position), (parts,), jnp.float32, least / len(shards), top_value / len(shards))
        return jnp.repeat(jnp.exp(heights), dims[position] // parts).reshape((-1,) + (1,) * (len(dims) - position - 1))

    factor_of = one(*shards[0])
    for cut in shards[1:]:
        factor_of = factor_of * one(*cut)
    return factor_of


def noise(own_key, dims, deviation, reach, split=(), kind=jnp.bfloat16):
    array = jax.random.normal(own_key, dims, jnp.float32) * deviation
    if len(split) > 0:
        array = levels(own_key, dims, split, -0.22, 0.18) * array
    return jnp.clip(array, min=-reach, max=reach).astype(kind)


def setup_inputs(seed: int = 0) -> dict:
    keys = jax.random.split(jax.random.key(seed), 30)
    grid_in = noise(keys[0], (MEMBERS, GRID, F_IN), 1.0, 6.0, ((0, 4), (1, 32)))
    mesh_embed = noise(keys[1], (MESH, D), 1.0, 6.0, ((0, 32),))
    g2m_src = plant(jax.random.randint(keys[2], (BANDS, BANDS, SLOTS), 0, G_DEV), jax.random.fold_in(keys[2], 1), 0, G_DEV - 1).astype(jnp.int32)
    g2m_dst = plant(jax.random.randint(keys[3], (BANDS, BANDS, SLOTS), 0, M_DEV), jax.random.fold_in(keys[3], 1), 0, M_DEV - 1).astype(jnp.int32)
    g2m_own_src = plant(jax.random.randint(keys[4], (BANDS, G2M_OWN), 0, G_DEV), jax.random.fold_in(keys[4], 1), 0, G_DEV - 1).astype(jnp.int32)
    g2m_own_dst = plant(jax.random.randint(keys[5], (BANDS, G2M_OWN), 0, M_DEV), jax.random.fold_in(keys[5], 1), 0, M_DEV - 1).astype(jnp.int32)
    g2m_len = draw_g2m_len(jax.random.fold_in(keys[29], 71), 0)
    mesh_nbr = draw_mesh_nbr(jax.random.fold_in(keys[29], 71), 0)
    halo_rows = plant(jax.random.randint(keys[8], (BANDS, HB), 0, M_DEV), jax.random.fold_in(keys[8], 1), 0, M_DEV - 1).astype(jnp.int32)
    m2g_src = plant(jax.random.randint(keys[9], (BANDS, BANDS, SLOTS), 0, M_DEV), jax.random.fold_in(keys[9], 1), 0, M_DEV - 1).astype(jnp.int32)
    m2g_dst = plant(jax.random.randint(keys[10], (BANDS, BANDS, SLOTS), 0, G_DEV), jax.random.fold_in(keys[10], 1), 0, G_DEV - 1).astype(jnp.int32)
    m2g_own_src = plant(jax.random.randint(keys[11], (BANDS, M2G_OWN), 0, M_DEV), jax.random.fold_in(keys[11], 1), 0, M_DEV - 1).astype(jnp.int32)
    m2g_own_dst = plant(jax.random.randint(keys[12], (BANDS, M2G_OWN), 0, G_DEV), jax.random.fold_in(keys[12], 1), 0, G_DEV - 1).astype(jnp.int32)
    m2g_len = draw_m2g_len(jax.random.fold_in(keys[29], 71), 0)
    w_embed = noise(keys[14], (F_IN, D), F_IN ** -0.5, 0.375)
    w_send = noise(keys[15], (D, D), D ** -0.5, 0.25)
    w_mesh = noise(keys[16], (D, D), D ** -0.5, 0.25)
    attn_gain = jnp.clip(1.0 + 0.18 * jax.random.normal(keys[17], (D,), jnp.float32), 0.1, 1.9)
    w_query = draw_w_query(jax.random.fold_in(keys[29], 71), 0)
    w_key = draw_w_key(jax.random.fold_in(keys[29], 71), 0)
    w_value = noise(keys[20], (D, D), D ** -0.5, 0.25, ((0, 4),))
    w_project = noise(keys[21], (D, D), D ** -0.5, 0.25, ((0, 4),))
    mlp_gain = jnp.clip(1.0 + 0.18 * jax.random.normal(keys[22], (D,), jnp.float32), 0.1, 1.9)
    w_up = noise(keys[23], (D, FFN), D ** -0.5, 0.25, ((0, 4),))
    w_down = noise(keys[24], (FFN, D), FFN ** -0.5, 0.125, ((0, 4),))
    w_return = noise(keys[25], (D, D), D ** -0.5, 0.25)
    w_grid = noise(keys[26], (D, D), D ** -0.5, 0.25)
    w_skip = noise(keys[27], (D, D), D ** -0.5, 0.25)
    w_out = noise(keys[28], (D, F_OUT), D ** -0.5, 0.25)
    return dict(grid_in=grid_in, mesh_embed=mesh_embed, g2m_src=g2m_src, g2m_dst=g2m_dst, g2m_own_src=g2m_own_src, g2m_own_dst=g2m_own_dst, g2m_len=g2m_len, mesh_nbr=mesh_nbr, halo_rows=halo_rows, m2g_src=m2g_src, m2g_dst=m2g_dst, m2g_own_src=m2g_own_src, m2g_own_dst=m2g_own_dst, m2g_len=m2g_len, w_embed=w_embed, w_send=w_send, w_mesh=w_mesh, attn_gain=attn_gain, w_query=w_query, w_key=w_key, w_value=w_value, w_project=w_project, mlp_gain=mlp_gain, w_up=w_up, w_down=w_down, w_return=w_return, w_grid=w_grid, w_skip=w_skip, w_out=w_out)


EPS = 1e-05

def layer_norm(values, norm_gain):
    centred = values - lax.optimization_barrier(jnp.mean(values, axis=-1, keepdims=True))
    spread = lax.optimization_barrier(jnp.mean(centred * centred, axis=-1, keepdims=True))
    return centred * lax.rsqrt(spread + EPS) * norm_gain

def edge_sum(table, src_local, dst_local, own_src, own_dst, lengths, src_rows, dst_rows):
    part_count = src_local.shape[0]
    sender = lax.broadcasted_iota(jnp.int32, src_local.shape, 0)
    target = lax.broadcasted_iota(jnp.int32, src_local.shape, 1)
    column = lax.broadcasted_iota(jnp.int32, src_local.shape, 2)
    source = (sender * src_rows + src_local).reshape(-1)
    landing = target * dst_rows + jnp.transpose(dst_local, (1, 0, 2))
    live_slot = (column < lengths[:, :, None]) & (sender != target)
    landing = jnp.where(live_slot, landing, part_count * dst_rows).reshape(-1)
    band = lax.broadcasted_iota(jnp.int32, own_src.shape, 0)
    own_column = lax.broadcasted_iota(jnp.int32, own_src.shape, 1)
    own_len = jnp.diagonal(lengths)
    own_source = (band * src_rows + own_src).reshape(-1)
    own_landing = jnp.where(own_column < own_len[:, None], band * dst_rows + own_dst, part_count * dst_rows).reshape(-1)
    all_source = jnp.concatenate([source, own_source]).astype(jnp.int32)
    all_landing = jnp.concatenate([landing, own_landing]).astype(jnp.int32)
    carried = table[all_source].astype(jnp.float32)
    summed = jax.ops.segment_sum(carried, all_landing, num_segments=part_count * dst_rows + 1)
    return summed[:part_count * dst_rows]

def attend_block(queries, label_block, key_rows, value_rows):
    block = queries.shape[0]
    slots = K_NBR + 1
    query_heads = queries.reshape(block, H, DH).astype(jnp.float32)
    key_heads = key_rows.reshape(block, slots, H, DH).astype(jnp.float32)
    value_heads = value_rows.reshape(block, slots, H, DH).astype(jnp.float32)
    scores = jnp.einsum('bhd,bkhd->bhk', query_heads, key_heads) / math.sqrt(DH)
    top_score = lax.optimization_barrier(jnp.max(scores, axis=-1, keepdims=True))
    weights = jnp.exp(scores - top_score)
    denom = lax.optimization_barrier(jnp.sum(weights, axis=-1, keepdims=True))
    same = label_block[:, :, None] == label_block[:, None, :]
    repeats = lax.optimization_barrier(jnp.sum(same.astype(jnp.float32), axis=2))
    before = lax.broadcasted_iota(jnp.int32, (1, slots, slots), 2) < lax.broadcasted_iota(jnp.int32, (1, slots, slots), 1)
    first = jnp.logical_not(jnp.any(same & before, axis=2))
    probs = (repeats[:, None, :] * weights / denom).astype(jnp.bfloat16)
    probs = jnp.where(first[:, None, :], probs, jnp.zeros_like(probs))
    mixed = jnp.einsum('bhk,bkhd->bhd', probs.astype(jnp.float32), value_heads)
    return mixed.reshape(block, D).astype(jnp.bfloat16)

def reference(grid_in, mesh_embed, g2m_src, g2m_dst, g2m_own_src, g2m_own_dst, g2m_len, mesh_nbr, halo_rows, m2g_src, m2g_dst, m2g_own_src, m2g_own_dst, m2g_len, w_embed, w_send, w_mesh, attn_gain, w_query, w_key, w_value, w_project, mlp_gain, w_up, w_down, w_return, w_grid, w_skip, w_out):
    halo_global = (jnp.arange(BANDS, dtype=jnp.int32)[:, None] * M_DEV + halo_rows).reshape(-1)
    node_ids = jnp.arange(MESH, dtype=jnp.int32)
    node_part = (node_ids // M_DEV)[:, None]
    remote_pos = jnp.clip(mesh_nbr - M_DEV, 0, BANDS * HB - 1)
    neighbour_global = jnp.where(mesh_nbr < M_DEV, node_part * M_DEV + mesh_nbr, halo_global[remote_pos])
    index_all = jnp.concatenate([node_ids[:, None], neighbour_global], axis=1).astype(jnp.int32)
    label_all = jnp.concatenate([(node_ids % M_DEV)[:, None], mesh_nbr], axis=1).astype(jnp.int32)
    block = min(512, M_DEV)
    count = MESH // block

    def one_member(member_in):
        grid_latent = jax.nn.silu(jnp.dot(member_in, w_embed, preferred_element_type=jnp.float32)).astype(jnp.bfloat16)
        send_rows = jnp.dot(grid_latent, w_send, preferred_element_type=jnp.float32).astype(jnp.bfloat16)
        mesh_agg = edge_sum(send_rows, g2m_src, g2m_dst, g2m_own_src, g2m_own_dst, g2m_len, G_DEV, M_DEV)
        update = jax.nn.silu(jnp.dot(mesh_agg.astype(jnp.bfloat16), w_mesh, preferred_element_type=jnp.float32))
        mesh_state = (mesh_embed.astype(jnp.float32) + update).astype(jnp.bfloat16)
        normed = layer_norm(mesh_state.astype(jnp.float32), attn_gain).astype(jnp.bfloat16)
        queries = jnp.dot(normed, w_query, preferred_element_type=jnp.float32).astype(jnp.bfloat16)
        key_all = jnp.dot(normed, w_key, preferred_element_type=jnp.float32).astype(jnp.bfloat16)
        value_all = jnp.dot(normed, w_value, preferred_element_type=jnp.float32).astype(jnp.bfloat16)

        def run_block(item):
            query_block, index_block, label_block = item
            return attend_block(query_block, label_block, key_all[index_block], value_all[index_block])
        attended = lax.map(run_block, (queries.reshape(count, block, D), index_all.reshape(count, block, K_NBR + 1), label_all.reshape(count, block, K_NBR + 1))).reshape(MESH, D)
        after_attn = mesh_state.astype(jnp.float32) + jnp.dot(attended, w_project, preferred_element_type=jnp.float32)
        normed_two = layer_norm(after_attn, mlp_gain).astype(jnp.bfloat16)
        expanded = jax.nn.silu(jnp.dot(normed_two, w_up, preferred_element_type=jnp.float32)).astype(jnp.bfloat16)
        mesh_out = (after_attn + jnp.dot(expanded, w_down, preferred_element_type=jnp.float32)).astype(jnp.bfloat16)
        return_rows = jnp.dot(mesh_out, w_return, preferred_element_type=jnp.float32).astype(jnp.bfloat16)
        grid_agg = edge_sum(return_rows, m2g_src, m2g_dst, m2g_own_src, m2g_own_dst, m2g_len, M_DEV, G_DEV)
        pre = jnp.dot(grid_agg.astype(jnp.bfloat16), w_grid, preferred_element_type=jnp.float32)
        pre = pre + jnp.dot(grid_latent, w_skip, preferred_element_type=jnp.float32)
        updated = jax.nn.silu(pre).astype(jnp.bfloat16)
        result = lax.dot_general(w_out, updated, (((0,), (1,)), ((), ())), preferred_element_type=jnp.float32)
        return result.astype(jnp.bfloat16)
    return lax.map(one_member, grid_in)
```

```python
import functools
import math

import jax
import jax.numpy as jnp
from jax import lax
from jax.experimental import pallas as pl
from jax.experimental.pallas import tpu as pltpu
from jax.sharding import PartitionSpec as P

DH = 128
EPS = 1e-05
BF = jnp.bfloat16
F32 = jnp.float32

ANY = pl.BlockSpec(memory_space=pl.ANY)
VMEM = pl.BlockSpec(memory_space=pltpu.VMEM)
SMEM = pl.BlockSpec(memory_space=pltpu.SMEM)


def dot(a, b):
    return jnp.dot(a, b, preferred_element_type=F32)


def dot_nt(a, b):
    return lax.dot_general(a, b, (((1,), (1,)), ((), ())), preferred_element_type=F32)


def silu(v):
    return v / (1.0 + jnp.exp(-v))


def hot_rows(row, count):
    ids = lax.broadcasted_iota(jnp.int32, (count, row.shape[1]), 0)
    return jnp.where(ids == row, 1.0, 0.0).astype(BF)


def live(row, length):
    slot = lax.broadcasted_iota(jnp.int32, row.shape, 1)
    return jnp.where(slot < length, row, -1)


def layer_norm(values, gain):
    centred = values - jnp.mean(values, axis=-1, keepdims=True)
    spread = jnp.mean(centred * centred, axis=-1, keepdims=True)
    return centred * lax.rsqrt(spread + EPS) * gain


def call(body, outs, ins, operands, scratch=(), flops=0, nbytes=0, name=None):
    return pl.pallas_call(
        body,
        out_shape=[jax.ShapeDtypeStruct(s, d) for s, d in outs],
        in_specs=ins,
        out_specs=[VMEM] * len(outs),
        scratch_shapes=list(scratch),
        name=name,
        cost_estimate=pl.CostEstimate(flops=flops, bytes_accessed=nbytes, transcendentals=0),
    )(*operands)


def around(bands):
    band = lax.axis_index("space")
    return band, jnp.minimum(band + 1, bands - 1), jnp.maximum(band - 1, 0)


def pick_body(
    bands, x_ref, src_ref, back_ref, wq, wk, wv, wp, wu, wd, up_ref, down_ref, a_ref, b_ref, sem
):
    band, upper, lower = around(bands)
    half = band % 2
    heads = wp.shape[0] // 2
    deep = wd.shape[0] // 2
    width = wp.shape[1]
    blocks = wu.shape[1] // width
    top = pl.multiple_of(half * heads, heads)
    low = pl.multiple_of(half * deep, deep)
    copies = []
    for i, w in enumerate((wq, wk, wv)):
        copies.append((w, a_ref.at[:, i * width : (i + 1) * width]))
    copies.append((wp.at[pl.ds(top, heads)], b_ref.at[0:heads]))
    copies.append((wd.at[pl.ds(low, deep)], b_ref.at[heads : heads + deep]))
    for i in range(blocks):
        at = heads + deep + i * heads
        copies.append(
            (wu.at[pl.ds(top, heads), i * width : (i + 1) * width], b_ref.at[at : at + heads])
        )
    copies = [pltpu.make_async_copy(s, d, sem.at[i]) for i, (s, d) in enumerate(copies)]
    for copy in copies:
        copy.start()
    x = x_ref[...]
    rows = x.shape[0]
    slots = src_ref.shape[1]
    eye = lax.broadcasted_iota(jnp.int32, (slots, slots), 0) == lax.broadcasted_iota(
        jnp.int32, (slots, slots), 1
    )
    for out, at in ((up_ref, upper), (down_ref, lower)):
        wanted = src_ref[pl.ds(at, 1), :].astype(F32)
        column = jnp.sum(jnp.where(eye, wanted, 0.0), axis=1, keepdims=True).astype(jnp.int32)
        ids = lax.broadcasted_iota(jnp.int32, (slots, rows), 1)
        picker = jnp.where(ids == column, 1.0, 0.0).astype(BF)
        out[0:slots, :] = dot(picker, x).astype(BF)
        back = back_ref[pl.ds(at, 1), :].astype(F32)
        out[slots:, :] = jnp.broadcast_to(back, (out.shape[0] - slots, slots)).astype(BF)
    for copy in copies:
        copy.wait()


def embed_body(bands, x_ref, we_ref, src_ref, dst_ref, len_ref, latent_ref, agg_ref):
    band, _, _ = around(bands)
    latent = silu(dot(x_ref[...], we_ref[...])).astype(BF)
    latent_ref[...] = latent
    mesh_rows = agg_ref.shape[0]
    src_hot = hot_rows(src_ref[...], x_ref.shape[0])
    dst_hot = hot_rows(live(dst_ref[...], len_ref[band]), mesh_rows)
    links = dot_nt(dst_hot, src_hot).astype(BF)
    agg_ref[...] = dot(links, latent)


def mesh_body(
    bands,
    agg_ref,
    below_ref,
    above_ref,
    dst_ref,
    len_ref,
    we_ref,
    ws_ref,
    wm_ref,
    static_ref,
    gain_ref,
    rows_ref,
    state_ref,
    normed_ref,
    halo_ref,
    wide,
    own,
):
    band, upper, lower = around(bands)
    total = agg_ref[...]
    mesh_rows = total.shape[0]
    slots = dst_ref.shape[1]
    for ref, at, there in ((below_ref, lower, band > 0), (above_ref, upper, band < bands - 1)):
        count = jnp.where(there, len_ref[at], 0)
        latent = silu(dot(ref[0:slots, :], we_ref[...])).astype(BF)
        dst_hot = hot_rows(live(dst_ref[pl.ds(at, 1), :], count), mesh_rows)
        total = total + dot(dst_hot, latent)
    agg = dot(total.astype(BF), ws_ref[...]).astype(BF)
    state = (static_ref[...].astype(F32) + silu(dot(agg, wm_ref[...]))).astype(BF)
    state_ref[...] = state
    normed = layer_norm(state.astype(F32), gain_ref[...]).astype(BF)
    normed_ref[...] = normed
    wide[...] = normed.astype(F32)
    published = own.shape[0]
    for j in range(published):
        own[j : j + 1, :] = wide[pl.ds(rows_ref[0, j], 1), :]
    halo = own[...].astype(BF)
    for b in range(bands):
        halo_ref[b * published : (b + 1) * published, :] = halo


def attend_body(
    normed_ref, far_ref, nbr_ref, wq, wk, wv, a1, a2, a3, out_ref, w_ref, rep_ref, sem
):
    me = lax.axis_index("member")
    part, width = wq.shape
    copies = []
    for i, w in enumerate((wq, wk, wv)):
        at = pl.multiple_of(me * part, part)
        copies.append((w, w_ref.at[pl.ds(at, part), i * width : (i + 1) * width]))
    for d, a in ((1, a1), (2, a2), (3, a3)):
        at = pl.multiple_of(((me - d) % 4) * part, part)
        copies.append((a, w_ref.at[pl.ds(at, part)]))
    copies = [pltpu.make_async_copy(s, d, sem.at[i]) for i, (s, d) in enumerate(copies)]
    for copy in copies:
        copy.start()
    normed = normed_ref[...]
    mesh_rows = normed.shape[0]
    table = mesh_rows + far_ref.shape[0]
    labels = jnp.transpose(nbr_ref[...], (1, 0))
    ids = lax.broadcasted_iota(jnp.int32, (mesh_rows, table), 1)
    rows = lax.broadcasted_iota(jnp.int32, (mesh_rows, 1), 0)
    repeats = jnp.where(ids == rows, 1.0, 0.0)
    for k in range(labels.shape[1]):
        repeats = repeats + jnp.where(ids == labels[:, k : k + 1], 1.0, 0.0)
    rep_ref[...] = repeats
    for copy in copies:
        copy.wait()
    own = dot(normed, w_ref[...]).astype(BF)
    far = dot(far_ref[...], w_ref[:, width:]).astype(BF)
    for h in range(width // DH):
        at = h * DH
        q = own[:, at : at + DH]
        k = jnp.concatenate(
            [own[:, width + at : width + at + DH], far[:, at : at + DH]], axis=0
        )
        v = jnp.concatenate(
            [own[:, 2 * width + at : 2 * width + at + DH], far[:, width + at : width + at + DH]],
            axis=0,
        )
        repeats = rep_ref[...]
        present = repeats > 0.0
        scores = jnp.where(present, dot_nt(q, k) / math.sqrt(DH), -jnp.inf)
        top = jnp.max(scores, axis=-1, keepdims=True)
        weights = repeats * jnp.exp(scores - top)
        probs = (weights / jnp.sum(weights, axis=-1, keepdims=True)).astype(BF)
        out_ref[:, at : at + DH] = dot(probs, v).astype(BF)


def mlp_body(
    att_ref,
    state_ref,
    gain_ref,
    wr_ref,
    wp,
    wu,
    wd,
    b1,
    b2,
    b3,
    s1,
    s2,
    s3,
    out_ref,
    p_ref,
    u_ref,
    d_ref,
    sem,
):
    me = lax.axis_index("member")
    half = lax.axis_index("space") % 2
    part, width = wp.shape
    deep = wd.shape[0]
    blocks = wu.shape[1] // width
    hp, hd = part // 2, deep // 2
    at_p = pl.multiple_of(me * part, part)
    at_d = pl.multiple_of(me * deep, deep)
    proj = [(wp, p_ref.at[pl.ds(at_p, part)])]
    up = [(wu, u_ref.at[pl.ds(at_p, part)])]
    down = [(wd, d_ref.at[pl.ds(at_d, deep)])]
    for d, b, s in ((1, b1, s1), (2, b2, s2), (3, b3, s3)):
        home = (me - d) % 4
        for ref, side in ((b, half), (s, 1 - half)):
            at_p = pl.multiple_of(home * part + side * hp, hp)
            at_d = pl.multiple_of(home * deep + side * hd, hd)
            proj.append((ref.at[0:hp], p_ref.at[pl.ds(at_p, hp)]))
            down.append((ref.at[hp : hp + hd], d_ref.at[pl.ds(at_d, hd)]))
            for i in range(blocks):
                at = hp + hd + i * hp
                up.append(
                    (
                        ref.at[at : at + hp],
                        u_ref.at[pl.ds(at_p, hp), i * width : (i + 1) * width],
                    )
                )
    count = 0
    groups = []
    for group in (proj, up, down):
        copies = []
        for s, d in group:
            copies.append(pltpu.make_async_copy(s, d, sem.at[count]))
            count += 1
        groups.append(copies)
        for copy in copies:
            copy.start()
    for copy in groups[0]:
        copy.wait()
    after = state_ref[...].astype(F32) + dot(att_ref[...], p_ref[...])
    normed = layer_norm(after, gain_ref[...]).astype(BF)
    for copy in groups[1]:
        copy.wait()
    expanded = silu(dot(normed, u_ref[...])).astype(BF)
    for copy in groups[2]:
        copy.wait()
    mesh_out = (after + dot(expanded, d_ref[...])).astype(BF)
    out_ref[...] = dot(mesh_out, wr_ref[...]).astype(BF)


def links_body(
    bands, rows, back_ref, src_ref, dst_ref, far_dst_ref, len_ref, below_ref, above_ref,
    latent_ref, ws_ref, lo_ref, hi_ref, grid_ref, pre_ref,
):
    band, upper, lower = around(bands)
    mesh_rows = back_ref.shape[0]
    slots = far_dst_ref.shape[1]
    pre_ref[...] = dot(latent_ref[...], ws_ref[...])
    src_hot = hot_rows(src_ref[...], mesh_rows)
    dst_hot = hot_rows(live(dst_ref[...], len_ref[band]), rows)
    links = dot_nt(dst_hot, src_hot).astype(BF)
    grid_ref[...] = dot(links, back_ref[...])
    for ref, out, at, there in (
        (below_ref, lo_ref, lower, band > 0),
        (above_ref, hi_ref, upper, band < bands - 1),
    ):
        count = jnp.where(there, len_ref[at], 0)
        src = ref[slots : slots + 1, :].astype(F32).astype(jnp.int32)
        src_hot = hot_rows(src, mesh_rows)
        dst_hot = hot_rows(live(far_dst_ref[pl.ds(at, 1), :], count), rows)
        out[...] = dot_nt(dst_hot, src_hot).astype(BF)


def final_body(grid_ref, pre_ref, lo_ref, hi_ref, below_ref, above_ref, wg_ref, wo_ref, out_ref):
    total = grid_ref[...] + dot(lo_ref[...], below_ref[...]) + dot(hi_ref[...], above_ref[...])
    updated = silu(dot(total.astype(BF), wg_ref[...]) + pre_ref[...]).astype(BF)
    out_ref[...] = dot_nt(wo_ref[...], updated).astype(BF)


def shards(
    grid_in,
    mesh_embed,
    g2m_src,
    g2m_dst,
    g2m_own_src,
    g2m_own_dst,
    g2m_len,
    mesh_nbr,
    halo_rows,
    m2g_src,
    m2g_dst,
    m2g_own_src,
    m2g_own_dst,
    m2g_len,
    w_embed,
    w_send,
    w_mesh,
    attn_gain,
    w_query,
    w_key,
    w_value,
    w_project,
    mlp_gain,
    w_up,
    w_down,
    w_return,
    w_grid,
    w_skip,
    w_out,
):
    x = grid_in[0]
    rows, channels = x.shape
    mesh_rows, width = mesh_embed.shape
    bands = lax.axis_size("space")
    slots = g2m_src.shape[2]
    part = w_query.shape[0]
    deep = w_down.shape[0]
    hidden = w_up.shape[1]
    published = halo_rows.shape[1]
    lane = -(-slots // 256) * 256
    g2m_count = g2m_len.reshape(-1)
    m2g_count = m2g_len.reshape(-1)
    bind = functools.partial

    up, down, pack_a, pack_b = call(
        bind(pick_body, bands),
        [
            ((slots + 16, channels), BF),
            ((slots + 16, channels), BF),
            ((part, 3 * width), BF),
            ((part // 2 + deep // 2 + part // 2 * (hidden // width), width), BF),
        ],
        [VMEM] * 3 + [ANY] * 6,
        (x, g2m_src[0], m2g_src[0], w_query, w_key, w_value, w_project, w_up, w_down),
        [pltpu.SemaphoreType.DMA((16,))],
        flops=int(3e8),
        nbytes=int(3e6),
        name="pick",
    )
    forward = [(i, i + 1) for i in range(bands - 1)]
    backward = [(i + 1, i) for i in range(bands - 1)]
    swap = [(i, i ^ 1) for i in range(bands)]

    def turn(block, d):
        return lax.ppermute(block, "member", [(i, (i + d) % 4) for i in range(4)])

    below = lax.ppermute(up, "space", forward)
    above = lax.ppermute(down, "space", backward)
    a1, a3, a2 = turn(pack_a, 1), turn(pack_a, 3), turn(pack_a, 2)
    latent, agg = call(
        bind(embed_body, bands),
        [((rows, width), BF), ((mesh_rows, width), F32)],
        [VMEM] * 4 + [SMEM],
        (x, w_embed, g2m_own_src, g2m_own_dst, g2m_count),
        flops=int(3e9),
        nbytes=int(3e6),
        name="embed",
    )
    pack_b, agg = lax.optimization_barrier((pack_b, agg))
    b1, b3, b2 = turn(pack_b, 1), turn(pack_b, 3), turn(pack_b, 2)
    state, normed, halo = call(
        bind(mesh_body, bands),
        [((mesh_rows, width), BF), ((mesh_rows, width), BF), ((bands * published, width), BF)],
        [VMEM] * 4 + [SMEM] + [VMEM] * 5 + [SMEM],
        (
            agg,
            below,
            above,
            g2m_dst[0],
            g2m_count,
            w_embed,
            w_send,
            w_mesh,
            mesh_embed,
            attn_gain.reshape(1, width),
            halo_rows,
        ),
        [pltpu.VMEM((mesh_rows, width), F32), pltpu.VMEM((published, width), F32)],
        flops=int(1e9),
        nbytes=int(3e6),
        name="mesh",
    )
    far = lax.all_to_all(halo, "space", 0, 0, tiled=True)
    (attended,) = call(
        attend_body,
        [((mesh_rows, width), BF)],
        [VMEM] * 3 + [ANY] * 6,
        (normed, far, mesh_nbr.T, w_query, w_key, w_value, a1, a2, a3),
        [
            pltpu.VMEM((width, 3 * width), BF),
            pltpu.VMEM((mesh_rows, mesh_rows + bands * published), F32),
            pltpu.SemaphoreType.DMA((8,)),
        ],
        flops=int(4e9),
        nbytes=int(4e6),
        name="attend",
    )
    s1, s2, s3 = (lax.ppermute(b, "space", swap) for b in (b1, b2, b3))
    (back,) = call(
        mlp_body,
        [((mesh_rows, width), BF)],
        [VMEM] * 4 + [ANY] * 9,
        (
            attended,
            state,
            mlp_gain.reshape(1, width),
            w_return,
            w_project,
            w_up,
            w_down,
            b1,
            b2,
            b3,
            s1,
            s2,
            s3,
        ),
        [
            pltpu.VMEM((4 * part, width), BF),
            pltpu.VMEM((4 * part, hidden), BF),
            pltpu.VMEM((4 * deep, width), BF),
            pltpu.SemaphoreType.DMA((48,)),
        ],
        flops=int(2e9),
        nbytes=int(6e6),
        name="mlp",
    )
    back_below = lax.ppermute(back, "space", forward)
    back_above = lax.ppermute(back, "space", backward)
    lo, hi, grid_agg, pre = call(
        bind(links_body, bands, rows),
        [
            ((rows, mesh_rows), BF),
            ((rows, mesh_rows), BF),
            ((rows, width), F32),
            ((rows, width), F32),
        ],
        [VMEM] * 4 + [SMEM] + [VMEM] * 4,
        (back, m2g_own_src, m2g_own_dst, m2g_dst[0], m2g_count, below, above, latent, w_skip),
        flops=int(4e9),
        nbytes=int(8e6),
        name="links",
    )
    (result,) = call(
        final_body,
        [((w_out.shape[1], rows), BF)],
        [VMEM] * 8,
        (grid_agg, pre, lo, hi, back_below, back_above, w_grid, w_out.T),
        flops=int(2e9),
        nbytes=int(8e6),
        name="final",
    )
    return result[None]


def solution(mesh):
    placed = (
        P("member", "space", None),
        P("space", None),
        P("space", None, None),
        P("space", None, None),
        P("space", None),
        P("space", None),
        P(None, "space"),
        P("space", None),
        P("space", None),
        P("space", None, None),
        P("space", None, None),
        P("space", None),
        P("space", None),
        P(None, "space"),
        P(),
        P(),
        P(),
        P(),
        P("member", None),
        P("member", None),
        P("member", None),
        P("member", None),
        P(),
        P("member", None),
        P("member", None),
        P(),
        P(),
        P(),
        P(),
    )
    return jax.shard_map(
        shards, mesh=mesh, in_specs=placed, out_specs=P("member", None, "space"), check_vma=False
    )
```

```python
import functools
import math

import jax
import jax.numpy as jnp
from jax import lax
from jax.experimental import pallas as pl
from jax.experimental.pallas import tpu as pltpu
from jax.sharding import PartitionSpec as P

DH = 128
EPS = 1e-05
BF = jnp.bfloat16
F32 = jnp.float32

HBM = pl.BlockSpec(memory_space=pltpu.HBM)
VMEM = pl.BlockSpec(memory_space=pltpu.VMEM)
SMEM = pl.BlockSpec(memory_space=pltpu.SMEM)


def dot(a, b):
    return jnp.dot(a, b, preferred_element_type=F32)


def dot_nt(a, b):
    return lax.dot_general(a, b, (((1,), (1,)), ((), ())), preferred_element_type=F32)


def silu(v):
    return v / (1.0 + jnp.exp(-v))


def hot_rows(row, count):
    ids = lax.broadcasted_iota(jnp.int32, (count, row.shape[1]), 0)
    return jnp.where(ids == row, 1.0, 0.0).astype(BF)


def live(row, length):
    slot = lax.broadcasted_iota(jnp.int32, row.shape, 1)
    return jnp.where(slot < length, row, -1)


def layer_norm(values, gain):
    centred = values - jnp.mean(values, axis=-1, keepdims=True)
    spread = jnp.mean(centred * centred, axis=-1, keepdims=True)
    return centred * lax.rsqrt(spread + EPS) * gain


def call(body, outs, operands, scratch=(), flops=0, nbytes=0, mib=24):
    specs = {"h": HBM, "v": VMEM, "d": VMEM, "s": SMEM}
    spaces = {"h": pltpu.HBM, "v": pltpu.VMEM}
    arrays = [
        pltpu.with_memory_space_constraint(a, spaces[w]) if w in spaces else a for w, a in operands
    ]
    kinds = {"h": pltpu.HBM, "v": pltpu.VMEM, "d": jax.ShapeDtypeStruct}
    shapes = [kinds[w](s, d) for w, s, d in outs]
    return pl.pallas_call(
        body,
        out_shape=shapes,
        in_specs=[specs[w] for w, _ in operands],
        out_specs=[specs[w] for w, _, _ in outs],
        scratch_shapes=list(scratch),
        compiler_params=pltpu.CompilerParams(vmem_limit_bytes=mib * 2**20),
        cost_estimate=pl.CostEstimate(flops=flops, bytes_accessed=nbytes, transcendentals=0),
    )(*arrays)


def around(bands):
    band = lax.axis_index("space")
    return band, jnp.minimum(band + 1, bands - 1), jnp.maximum(band - 1, 0)


def pick_body(
    bands, x_hbm, src_hbm, back_hbm, wq, wk, wv, wp, wu, wd, we_hbm, own_hbm, land_hbm,
    up_ref, down_ref, pack_ref, x_ref, we_ref, own_ref, land_ref, src_ref, back_ref, sem,
):
    band, upper, lower = around(bands)
    half = band % 2
    copies = [(src_hbm, src_ref), (back_hbm, back_ref), (x_hbm, x_ref)]
    copies += half_weights((wq, wk, wv, wp), wu, wd, half, pack_ref)
    copies += [(we_hbm, we_ref), (own_hbm, own_ref), (land_hbm, land_ref)]
    copies = start_all(copies, sem)
    for copy in copies[:3]:
        copy.wait()
    x = x_ref[...]
    rows = x.shape[0]
    slots = src_ref.shape[1]
    eye = lax.broadcasted_iota(jnp.int32, (slots, slots), 0) == lax.broadcasted_iota(
        jnp.int32, (slots, slots), 1
    )
    for out, at in ((up_ref, upper), (down_ref, lower)):
        wanted = src_ref[pl.ds(at, 1), :].astype(F32)
        column = jnp.sum(jnp.where(eye, wanted, 0.0), axis=1, keepdims=True).astype(jnp.int32)
        ids = lax.broadcasted_iota(jnp.int32, (slots, rows), 1)
        picker = jnp.where(ids == column, 1.0, 0.0).astype(BF)
        out[0:slots, :] = dot(picker, x).astype(BF)
        back = back_ref[pl.ds(at, 1), :].astype(F32)
        out[slots:, :] = jnp.broadcast_to(back, (out.shape[0] - slots, slots)).astype(BF)
    for copy in copies[3:]:
        copy.wait()


def start_all(pairs, sem, first=0):
    copies = [pltpu.make_async_copy(s, d, sem.at[first + i]) for i, (s, d) in enumerate(pairs)]
    for copy in copies:
        copy.start()
    return copies


def half_weights(square, wu, wd, half, pack_ref):
    _, piece, width = pack_ref.shape
    top = pl.multiple_of(half * piece, piece)
    deep = wd.shape[0] // 2
    count = len(square)
    pairs = [(w.at[pl.ds(top, piece)], pack_ref.at[i]) for i, w in enumerate(square)]
    pairs.append((wd.at[pl.ds(half * deep, deep)], pack_ref.at[count : count + deep]))
    for i in range(wu.shape[1] // width):
        pairs.append(
            (
                wu.at[pl.ds(top, piece), i * width : (i + 1) * width],
                pack_ref.at[count + deep + i],
            )
        )
    return pairs


def embed_body(bands, count, x_ref, we_ref, src_ref, dst_ref, len_ref, *refs):
    far, (latent_hbm, agg_ref), near, (latent_ref, sem) = (
        refs[:count],
        refs[count : count + 2],
        refs[count + 2 : -2],
        refs[-2:],
    )
    copies = start_all(list(zip(far, near)), sem)
    band, _, _ = around(bands)
    latent = silu(dot(x_ref[...], we_ref[...])).astype(BF)
    latent_ref[...] = latent
    copies += start_all([(latent_ref, latent_hbm)], sem, count)
    mesh_rows = agg_ref.shape[0]
    src_hot = hot_rows(src_ref[...], x_ref.shape[0])
    dst_hot = hot_rows(live(dst_ref[...], len_ref[band]), mesh_rows)
    links = dot_nt(dst_hot, src_hot).astype(BF)
    agg_ref[...] = dot(links, latent)
    for copy in copies:
        copy.wait()


def mesh_body(
    bands,
    agg_ref,
    below_ref,
    above_ref,
    dst_ref,
    len_ref,
    we_ref,
    ws_ref,
    wm_ref,
    static_ref,
    gain_ref,
    rows_ref,
    state_ref,
    normed_ref,
    halo_ref,
    wide,
    own,
):
    band, upper, lower = around(bands)
    total = agg_ref[...]
    mesh_rows = total.shape[0]
    slots = dst_ref.shape[1]
    for ref, at, there in ((below_ref, lower, band > 0), (above_ref, upper, band < bands - 1)):
        count = jnp.where(there, len_ref[at], 0)
        latent = silu(dot(ref[0:slots, :], we_ref[...])).astype(BF)
        dst_hot = hot_rows(live(dst_ref[pl.ds(at, 1), :], count), mesh_rows)
        total = total + dot(dst_hot, latent)
    agg = dot(total.astype(BF), ws_ref[...]).astype(BF)
    state = (static_ref[...].astype(F32) + silu(dot(agg, wm_ref[...]))).astype(BF)
    state_ref[...] = state
    normed = layer_norm(state.astype(F32), gain_ref[...]).astype(BF)
    normed_ref[...] = normed
    wide[...] = normed.astype(F32)
    published = own.shape[0]
    for j in range(published):
        own[j : j + 1, :] = wide[pl.ds(rows_ref[0, j], 1), :]
    halo = own[...].astype(BF)
    for b in range(bands):
        halo_ref[b * published : (b + 1) * published, :] = halo


def fill_body(
    bands, src_ref, dst_ref, far_dst_ref, len_ref, below_ref, above_ref, nbr_ref,
    links_hbm, rep_ref, links_ref, sem,
):
    band, upper, lower = around(bands)
    mesh_rows, table = rep_ref.shape
    rows = links_ref.shape[1]
    slots = far_dst_ref.shape[1]
    src_hot = hot_rows(src_ref[...], mesh_rows)
    dst_hot = hot_rows(live(dst_ref[...], len_ref[band]), rows)
    links_ref[0] = dot_nt(dst_hot, src_hot).astype(BF)
    for i, (ref, at, there) in enumerate(
        ((below_ref, lower, band > 0), (above_ref, upper, band < bands - 1))
    ):
        count = jnp.where(there, len_ref[at], 0)
        src = ref[slots : slots + 1, :].astype(F32).astype(jnp.int32)
        src_hot = hot_rows(src, mesh_rows)
        dst_hot = hot_rows(live(far_dst_ref[pl.ds(at, 1), :], count), rows)
        links_ref[i + 1] = dot_nt(dst_hot, src_hot).astype(BF)
    copies = start_all([(links_ref, links_hbm)], sem)
    labels = jnp.transpose(nbr_ref[...], (1, 0))
    ids = lax.broadcasted_iota(jnp.int32, (mesh_rows, table), 1)
    own = lax.broadcasted_iota(jnp.int32, (mesh_rows, 1), 0)
    repeats = jnp.where(ids == own, 1.0, 0.0)
    for k in range(labels.shape[1]):
        repeats = repeats + jnp.where(ids == labels[:, k : k + 1], 1.0, 0.0)
    rep_ref[...] = repeats
    for copy in copies:
        copy.wait()


def layer_body(
    normed_ref, far_ref, rep_ref, state_ref, gain_hbm, wr_hbm, wg_hbm, wq, wk, wv, wp, wu, wd,
    b1, b2, b3, s1, s2, s3, out_ref, m_ref, u_ref, d_ref, att_ref, gain_ref, wr_ref, wg_ref, sem,
):
    me = lax.axis_index("member")
    half = lax.axis_index("space") % 2
    square = (wq, wk, wv, wp)
    count = len(square)
    part, width = wq.shape
    piece = part // 2
    deep = wd.shape[0] // 2
    blocks = wu.shape[1] // width
    home = pl.multiple_of(me * part, part)
    heads = [(w, m_ref.at[i, pl.ds(home, part)]) for i, w in enumerate(square)]
    ups = [
        (wu.at[:, i * width : (i + 1) * width], u_ref.at[i, pl.ds(home, part)])
        for i in range(blocks)
    ]
    downs = [(wd, d_ref.at[pl.ds(me * 2 * deep, 2 * deep)])]
    for d, b, s in ((1, b1, s1), (3, b3, s3), (2, b2, s2)):
        source = (me - d) % 4
        for ref, side in ((b, half), (s, 1 - half)):
            at = pl.multiple_of(source * part + side * piece, piece)
            low = (source * 2 + side) * deep
            heads.append((ref.at[0:count], m_ref.at[:, pl.ds(at, piece)]))
            ups.append((ref.at[count + deep :], u_ref.at[:, pl.ds(at, piece)]))
            downs.append((ref.at[count : count + deep], d_ref.at[pl.ds(low, deep)]))
    heads = start_all(heads, sem)
    ups = start_all(ups, sem, len(heads))
    downs += [(wr_hbm, wr_ref), (wg_hbm, wg_ref)]
    heads_gain = start_all([(gain_hbm, gain_ref)], sem, len(heads) + len(ups) + len(downs))
    downs = start_all(downs, sem, len(heads) + len(ups))
    for copy in heads + heads_gain:
        copy.wait()
    normed = normed_ref[...]
    far = far_ref[...]
    queries = dot(normed, m_ref[0]).astype(BF)
    keys = jnp.concatenate([dot(normed, m_ref[1]).astype(BF), dot(far, m_ref[1]).astype(BF)], 0)
    values = jnp.concatenate([dot(normed, m_ref[2]).astype(BF), dot(far, m_ref[2]).astype(BF)], 0)
    for h in range(width // DH):
        at = slice(h * DH, (h + 1) * DH)
        repeats = rep_ref[...]
        scores = dot_nt(queries[:, at], keys[:, at]) / math.sqrt(DH)
        scores = jnp.where(repeats > 0.0, scores, -jnp.inf)
        top = jnp.max(scores, axis=-1, keepdims=True)
        weights = repeats * jnp.exp(scores - top)
        probs = (weights / jnp.sum(weights, axis=-1, keepdims=True)).astype(BF)
        att_ref[:, at] = dot(probs, values[:, at]).astype(BF)
    after = state_ref[...].astype(F32) + dot(att_ref[...], m_ref[3])
    normed = layer_norm(after, gain_ref[...]).astype(BF)
    for copy in ups + downs:
        copy.wait()
    total = after
    span = width // piece
    for i in range(blocks):
        expanded = silu(dot(normed, u_ref[i])).astype(BF)
        down = d_ref[i * span : (i + 1) * span].reshape(width, width)
        total = total + dot(expanded, down)
    back = dot(total.astype(BF), wr_ref[...]).astype(BF)
    out_ref[...] = dot(back, wg_ref[...]).astype(BF)


def part_body(
    back_ref, links_hbm, latent_hbm, ws_hbm, wo_hbm,
    out_ref, far_ref, wo_ref, own_ref, latent_ref, ws_ref, sem,
):
    copies = [(latent_hbm, latent_ref), (ws_hbm, ws_ref), (links_hbm.at[0], own_ref)]
    copies += [(links_hbm.at[1:3], far_ref), (wo_hbm, wo_ref)]
    copies = start_all(copies, sem)
    copies[0].wait()
    copies[1].wait()
    total = dot(latent_ref[...], ws_ref[...])
    copies[2].wait()
    out_ref[...] = total + dot(own_ref[...], back_ref[...])
    copies[3].wait()
    copies[4].wait()


def final_body(part_ref, links_ref, below_ref, above_ref, wo_ref, out_ref):
    total = part_ref[...] + dot(links_ref[0], below_ref[...])
    total = total + dot(links_ref[1], above_ref[...])
    out_ref[...] = dot_nt(wo_ref[...], silu(total).astype(BF)).astype(BF)


def shards(
    grid_in,
    mesh_embed,
    g2m_src,
    g2m_dst,
    g2m_own_src,
    g2m_own_dst,
    g2m_len,
    mesh_nbr,
    halo_rows,
    m2g_src,
    m2g_dst,
    m2g_own_src,
    m2g_own_dst,
    m2g_len,
    w_embed,
    w_send,
    w_mesh,
    attn_gain,
    w_query,
    w_key,
    w_value,
    w_project,
    mlp_gain,
    w_up,
    w_down,
    w_return,
    w_grid,
    w_skip,
    w_out,
):
    x = grid_in[0]
    rows, channels = x.shape
    mesh_rows, width = mesh_embed.shape
    bands = lax.axis_size("space")
    slots = g2m_src.shape[2]
    part = w_query.shape[0]
    piece = part // 2
    hidden = w_up.shape[1]
    published = halo_rows.shape[1]
    table = mesh_rows + bands * published
    g2m_count = g2m_len.reshape(-1)
    m2g_count = m2g_len.reshape(-1)
    w_deep = w_down.reshape(-1, piece, width)
    deep = w_deep.shape[0] // 2
    blocks = hidden // width
    square = (w_query, w_key, w_value, w_project)
    bind = functools.partial
    forward = [(i, i + 1) for i in range(bands - 1)]
    backward = [(i + 1, i) for i in range(bands - 1)]
    swap = [(i, i ^ 1) for i in range(bands)]

    def turn(block, d):
        return lax.ppermute(block, "member", [(i, (i + d) % 4) for i in range(4)])

    def like(a):
        return "v", a.shape, a.dtype

    def tag(where, *arrays):
        return [(where, a) for a in arrays]

    up, down, pack, x, w_embed, g2m_own_src, g2m_own_dst = call(
        bind(pick_body, bands),
        [
            ("v", (slots + 16, channels), BF),
            ("v", (slots + 16, channels), BF),
            ("v", (4 + deep + blocks, piece, width), BF),
            *map(like, (x, w_embed, g2m_own_src, g2m_own_dst)),
        ],
        tag("h", x, g2m_src[0], m2g_src[0], *square, w_up, w_deep, w_embed, g2m_own_src)
        + tag("h", g2m_own_dst),
        [
            pltpu.VMEM(g2m_src.shape[1:], jnp.int32),
            pltpu.VMEM(m2g_src.shape[1:], jnp.int32),
            pltpu.SemaphoreType.DMA((20,)),
        ],
        flops=int(3e8),
        nbytes=int(3e6),
    )
    below = lax.ppermute(up, "space", forward)
    above = lax.ppermute(down, "space", backward)
    b1, b3, b2 = turn(pack, 1), turn(pack, 3), turn(pack, 2)
    ahead = [
        g2m_dst[0],
        w_send,
        w_mesh,
        mesh_embed,
        attn_gain.reshape(1, width),
        m2g_own_src,
        m2g_own_dst,
        m2g_dst[0],
        mesh_nbr.T,
    ]
    latent, agg, *ahead = call(
        bind(embed_body, bands, len(ahead)),
        [("h", (rows, width), BF), ("v", (mesh_rows, width), F32), *map(like, ahead)],
        tag("v", x, w_embed, g2m_own_src, g2m_own_dst) + tag("s", g2m_count) + tag("h", *ahead),
        [pltpu.VMEM((rows, width), BF), pltpu.SemaphoreType.DMA((len(ahead) + 1,))],
        flops=int(3e9),
        nbytes=int(3e6),
    )
    state, normed, halo = call(
        bind(mesh_body, bands),
        [
            ("v", (mesh_rows, width), BF),
            ("v", (mesh_rows, width), BF),
            ("d", (bands * published, width), BF),
        ],
        tag("v", agg)
        + tag("d", below, above)
        + tag("v", ahead[0])
        + tag("s", g2m_count)
        + tag("v", w_embed, *ahead[1:5])
        + tag("s", halo_rows),
        [pltpu.VMEM((mesh_rows, width), F32), pltpu.VMEM((published, width), F32)],
        flops=int(1e9),
        nbytes=int(3e6),
    )
    far = lax.all_to_all(halo, "space", 0, 0, tiled=True)
    links, repeats = call(
        bind(fill_body, bands),
        [("h", (3, rows, mesh_rows), BF), ("v", (mesh_rows, table), F32)],
        tag("v", *ahead[5:8])
        + tag("s", m2g_count)
        + tag("d", below, above)
        + tag("v", ahead[8]),
        [pltpu.VMEM((3, rows, mesh_rows), BF), pltpu.SemaphoreType.DMA((1,))],
        flops=int(4e9),
        nbytes=int(8e6),
    )
    s1, s3, s2 = (lax.ppermute(b, "space", swap) for b in (b1, b3, b2))
    (back,) = call(
        layer_body,
        [("v", (mesh_rows, width), BF)],
        tag("v", normed)
        + tag("d", far)
        + tag("v", repeats, state)
        + tag("h", mlp_gain.reshape(1, width), w_return, w_grid)
        + tag("h", *square, w_up, w_deep, b1, b2, b3, s1, s2, s3),
        [
            pltpu.VMEM((4, 4 * part, width), BF),
            pltpu.VMEM((blocks, 4 * part, width), BF),
            pltpu.VMEM((8 * deep, piece, width), BF),
            pltpu.VMEM((mesh_rows, width), BF),
            pltpu.VMEM((1, width), F32),
            pltpu.VMEM((width, width), BF),
            pltpu.VMEM((width, width), BF),
            pltpu.SemaphoreType.DMA((40,)),
        ],
        flops=int(5e9),
        nbytes=int(6e6),
    )
    back_below = lax.ppermute(back, "space", forward)
    back_above = lax.ppermute(back, "space", backward)
    part, far_links, w_last = call(
        part_body,
        [("v", (rows, width), F32), ("v", (2, rows, mesh_rows), BF), like(w_out.T)],
        tag("v", back) + tag("h", links, latent, w_skip, w_out.T),
        [
            pltpu.VMEM((rows, mesh_rows), BF),
            pltpu.VMEM((rows, width), BF),
            pltpu.VMEM((width, width), BF),
            pltpu.SemaphoreType.DMA((5,)),
        ],
        flops=int(1e9),
        nbytes=int(2e6),
    )
    (result,) = call(
        final_body,
        [("d", (w_out.shape[1], rows), BF)],
        tag("v", part, far_links) + tag("d", back_below, back_above) + tag("v", w_last),
        flops=int(2e9),
        nbytes=int(8e6),
    )
    return result[None]


def solution(mesh):
    placed = (
        P("member", "space", None),
        P("space", None),
        P("space", None, None),
        P("space", None, None),
        P("space", None),
        P("space", None),
        P(None, "space"),
        P("space", None),
        P("space", None),
        P("space", None, None),
        P("space", None, None),
        P("space", None),
        P("space", None),
        P(None, "space"),
        P(),
        P(),
        P(),
        P(),
        P("member", None),
        P("member", None),
        P("member", None),
        P("member", None),
        P(),
        P("member", None),
        P("member", None),
        P(),
        P(),
        P(),
        P(),
    )
    return jax.shard_map(
        shards, mesh=mesh, in_specs=placed, out_specs=P("member", None, "space"), check_vma=False
    )
```

```python
import functools
import math

import jax
import jax.numpy as jnp
from jax import lax
from jax.experimental import pallas as pl
from jax.experimental.pallas import tpu as pltpu
from jax.sharding import PartitionSpec as P

DH = 128
EPS = 1e-05
BF = jnp.bfloat16
F32 = jnp.float32

HBM = pl.BlockSpec(memory_space=pltpu.HBM)
VMEM = pl.BlockSpec(memory_space=pltpu.VMEM)
SMEM = pl.BlockSpec(memory_space=pltpu.SMEM)


def dot(a, b):
    return jnp.dot(a, b, preferred_element_type=F32)


def dot_nt(a, b):
    return lax.dot_general(a, b, (((1,), (1,)), ((), ())), preferred_element_type=F32)


def silu(v):
    return v / (1.0 + jnp.exp(-v))


def hot_rows(row, count):
    ids = lax.broadcasted_iota(jnp.int32, (count, row.shape[1]), 0)
    return jnp.where(ids == row, 1.0, 0.0).astype(BF)


def live(row, length):
    slot = lax.broadcasted_iota(jnp.int32, row.shape, 1)
    return jnp.where(slot < length, row, -1)


def layer_norm(values, gain):
    centred = values - jnp.mean(values, axis=-1, keepdims=True)
    spread = jnp.mean(centred * centred, axis=-1, keepdims=True)
    return centred * lax.rsqrt(spread + EPS) * gain


def call(body, outs, operands, scratch=(), flops=0, nbytes=0, mib=24):
    specs = {"h": HBM, "v": VMEM, "d": VMEM, "s": SMEM}
    spaces = {"h": pltpu.HBM, "v": pltpu.VMEM}
    arrays = [
        pltpu.with_memory_space_constraint(a, spaces[w]) if w in spaces else a for w, a in operands
    ]
    kinds = {"h": pltpu.HBM, "v": pltpu.VMEM, "d": jax.ShapeDtypeStruct}
    shapes = [kinds[w](s, d) for w, s, d in outs]
    return pl.pallas_call(
        body,
        out_shape=shapes,
        in_specs=[specs[w] for w, _ in operands],
        out_specs=[specs[w] for w, _, _ in outs],
        scratch_shapes=list(scratch),
        compiler_params=pltpu.CompilerParams(vmem_limit_bytes=mib * 2**20),
        cost_estimate=pl.CostEstimate(flops=flops, bytes_accessed=nbytes, transcendentals=0),
    )(*arrays)


def around(bands):
    band = lax.axis_index("space")
    odd = band % 2
    cross = band - 1 + 2 * odd
    there = (cross >= 0) & (cross < bands)
    return band, band + 1 - 2 * odd, jnp.clip(cross, 0, bands - 1), there


def pick_body(
    bands, x_hbm, src_hbm, back_hbm, wq, wk, wv, wp, wu, wd, we_hbm, own_hbm, land_hbm,
    near_ref, cross_ref, a_ref, b_ref, x_ref, we_ref, own_ref, land_ref, src_ref, back_ref, sem,
):
    band, near, cross, _ = around(bands)
    copies = [(src_hbm, src_ref), (back_hbm, back_ref), (x_hbm, x_ref)]
    copies += half_weights((wq, wk, wv, wp), wu, wd, band % 2, a_ref, b_ref)
    copies += [(we_hbm, we_ref), (own_hbm, own_ref), (land_hbm, land_ref)]
    copies = start_all(copies, sem)
    for copy in copies[:3]:
        copy.wait()
    x = x_ref[...]
    rows = x.shape[0]
    slots = src_ref.shape[1]
    eye = lax.broadcasted_iota(jnp.int32, (slots, slots), 0) == lax.broadcasted_iota(
        jnp.int32, (slots, slots), 1
    )
    for out, at in ((near_ref, near), (cross_ref, cross)):
        wanted = src_ref[pl.ds(at, 1), :].astype(F32)
        column = jnp.sum(jnp.where(eye, wanted, 0.0), axis=1, keepdims=True).astype(jnp.int32)
        ids = lax.broadcasted_iota(jnp.int32, (slots, rows), 1)
        picker = jnp.where(ids == column, 1.0, 0.0).astype(BF)
        out[0:slots, :] = dot(picker, x).astype(BF)
        back = back_ref[pl.ds(at, 1), :].astype(F32)
        out[slots:, :] = jnp.broadcast_to(back, (out.shape[0] - slots, slots)).astype(BF)
    for copy in copies[3:]:
        copy.wait()


def start_all(pairs, sem, first=0):
    copies = [pltpu.make_async_copy(s, d, sem.at[first + i]) for i, (s, d) in enumerate(pairs)]
    for copy in copies:
        copy.start()
    return copies


def half_weights(square, wu, wd, half, a_ref, b_ref):
    _, piece, width = a_ref.shape
    top = pl.multiple_of(half * piece, piece)
    deep = wd.shape[0] // 4
    low = half * 2 * deep
    count = len(square)
    pairs = [(w.at[pl.ds(top, piece)], a_ref.at[i]) for i, w in enumerate(square)]
    pairs.append((wd.at[pl.ds(low, deep)], a_ref.at[count:]))
    pairs.append((wd.at[pl.ds(low + deep, deep)], b_ref.at[0:deep]))
    for i in range(wu.shape[1] // width):
        pairs.append(
            (wu.at[pl.ds(top, piece), i * width : (i + 1) * width], b_ref.at[deep + i])
        )
    return pairs


def embed_body(count, x_ref, we_ref, src_ref, dst_ref, len_ref, *refs):
    far, (latent_hbm, agg_ref), near, (latent_ref, sem) = (
        refs[:count],
        refs[count : count + 2],
        refs[count + 2 : -2],
        refs[-2:],
    )
    copies = start_all(list(zip(far, near)), sem)
    band = lax.axis_index("space")
    latent = silu(dot(x_ref[...], we_ref[...])).astype(BF)
    latent_ref[...] = latent
    copies += start_all([(latent_ref, latent_hbm)], sem, count)
    mesh_rows = agg_ref.shape[0]
    src_hot = hot_rows(src_ref[...], x_ref.shape[0])
    dst_hot = hot_rows(live(dst_ref[...], len_ref[band]), mesh_rows)
    links = dot_nt(dst_hot, src_hot).astype(BF)
    agg_ref[...] = dot(links, latent)
    for copy in copies:
        copy.wait()


def mesh_body(
    bands,
    agg_ref,
    near_ref,
    cross_ref,
    dst_ref,
    len_ref,
    we_ref,
    ws_ref,
    wm_ref,
    static_ref,
    gain_ref,
    rows_ref,
    state_ref,
    normed_ref,
    halo_ref,
    wide,
    own,
):
    _, near, cross, there = around(bands)
    total = agg_ref[...]
    mesh_rows = total.shape[0]
    slots = dst_ref.shape[1]
    for ref, at, some in ((near_ref, near, True), (cross_ref, cross, there)):
        count = jnp.where(some, len_ref[at], 0)
        latent = silu(dot(ref[0:slots, :], we_ref[...])).astype(BF)
        dst_hot = hot_rows(live(dst_ref[pl.ds(at, 1), :], count), mesh_rows)
        total = total + dot(dst_hot, latent)
    agg = dot(total.astype(BF), ws_ref[...]).astype(BF)
    state = (static_ref[...].astype(F32) + silu(dot(agg, wm_ref[...]))).astype(BF)
    state_ref[...] = state
    normed = layer_norm(state.astype(F32), gain_ref[...]).astype(BF)
    normed_ref[...] = normed
    wide[...] = normed.astype(F32)
    published = own.shape[0]
    for j in range(published):
        own[j : j + 1, :] = wide[pl.ds(rows_ref[0, j], 1), :]
    halo = own[...].astype(BF)
    for b in range(bands):
        halo_ref[b * published : (b + 1) * published, :] = halo


def fill_body(
    bands, src_ref, dst_ref, far_dst_ref, len_ref, near_ref, cross_ref, nbr_ref,
    links_hbm, rep_ref, links_ref, sem,
):
    band, near, cross, there = around(bands)
    mesh_rows, table = rep_ref.shape
    rows = links_ref.shape[1]
    slots = far_dst_ref.shape[1]
    src_hot = hot_rows(src_ref[...], mesh_rows)
    dst_hot = hot_rows(live(dst_ref[...], len_ref[band]), rows)
    links_ref[0] = dot_nt(dst_hot, src_hot).astype(BF)
    for i, (ref, at, some) in enumerate(((near_ref, near, True), (cross_ref, cross, there))):
        count = jnp.where(some, len_ref[at], 0)
        src = ref[slots : slots + 1, :].astype(F32).astype(jnp.int32)
        src_hot = hot_rows(src, mesh_rows)
        dst_hot = hot_rows(live(far_dst_ref[pl.ds(at, 1), :], count), rows)
        links_ref[i + 1] = dot_nt(dst_hot, src_hot).astype(BF)
    copies = start_all([(links_ref, links_hbm)], sem)
    labels = jnp.transpose(nbr_ref[...], (1, 0))
    ids = lax.broadcasted_iota(jnp.int32, (mesh_rows, table), 1)
    own = lax.broadcasted_iota(jnp.int32, (mesh_rows, 1), 0)
    repeats = jnp.where(ids == own, 1.0, 0.0)
    for k in range(labels.shape[1]):
        repeats = repeats + jnp.where(ids == labels[:, k : k + 1], 1.0, 0.0)
    rep_ref[...] = repeats
    for copy in copies:
        copy.wait()


def layer_body(
    normed_ref, far_ref, rep_ref, state_ref, gain_hbm, wr_hbm, wg_hbm, wq, wk, wv, wp, wu, wd, *refs
):
    pieces, refs = refs[:12], refs[12:]
    out_ref, m_ref, u_ref, d_ref, att_ref, gain_ref, wr_ref, wg_ref, sem = refs
    me = lax.axis_index("member")
    half = lax.axis_index("space") % 2
    square = (wq, wk, wv, wp)
    count = len(square)
    part, width = wq.shape
    piece = part // 2
    deep = wd.shape[0] // 4
    blocks = wu.shape[1] // width
    home = pl.multiple_of(me * part, part)
    heads = [(w, m_ref.at[i, pl.ds(home, part)]) for i, w in enumerate(square)]
    ups = [
        (wu.at[:, i * width : (i + 1) * width], u_ref.at[i, pl.ds(home, part)])
        for i in range(blocks)
    ]
    downs = [(wd, d_ref.at[pl.ds(me * 4 * deep, 4 * deep)])]
    for j, d in enumerate((1, 3, 2)):
        source = me ^ d
        for side, (a, b) in ((half, pieces[2 * j : 2 * j + 2]), (1 - half, pieces[2 * j + 6 : 2 * j + 8])):
            at = pl.multiple_of(source * part + side * piece, piece)
            low = (source * 2 + side) * 2 * deep
            heads.append((a.at[0:count], m_ref.at[:, pl.ds(at, piece)]))
            ups.append((b.at[deep:], u_ref.at[:, pl.ds(at, piece)]))
            downs.append((a.at[count:], d_ref.at[pl.ds(low, deep)]))
            downs.append((b.at[0:deep], d_ref.at[pl.ds(low + deep, deep)]))
    heads = start_all(heads, sem)
    ups = start_all(ups, sem, len(heads))
    downs += [(wr_hbm, wr_ref), (wg_hbm, wg_ref)]
    heads_gain = start_all([(gain_hbm, gain_ref)], sem, len(heads) + len(ups) + len(downs))
    downs = start_all(downs, sem, len(heads) + len(ups))
    for copy in heads + heads_gain:
        copy.wait()
    normed = normed_ref[...]
    far = far_ref[...]
    queries = dot(normed, m_ref[0]).astype(BF)
    keys = jnp.concatenate([dot(normed, m_ref[1]).astype(BF), dot(far, m_ref[1]).astype(BF)], 0)
    values = jnp.concatenate([dot(normed, m_ref[2]).astype(BF), dot(far, m_ref[2]).astype(BF)], 0)
    for h in range(width // DH):
        at = slice(h * DH, (h + 1) * DH)
        repeats = rep_ref[...]
        scores = dot_nt(queries[:, at], keys[:, at]) / math.sqrt(DH)
        scores = jnp.where(repeats > 0.0, scores, -jnp.inf)
        top = jnp.max(scores, axis=-1, keepdims=True)
        weights = repeats * jnp.exp(scores - top)
        probs = (weights / jnp.sum(weights, axis=-1, keepdims=True)).astype(BF)
        att_ref[:, at] = dot(probs, values[:, at]).astype(BF)
    after = state_ref[...].astype(F32) + dot(att_ref[...], m_ref[3])
    normed = layer_norm(after, gain_ref[...]).astype(BF)
    for copy in ups + downs:
        copy.wait()
    total = after
    span = width // piece
    for i in range(blocks):
        expanded = silu(dot(normed, u_ref[i])).astype(BF)
        down = d_ref[i * span : (i + 1) * span].reshape(width, width)
        total = total + dot(expanded, down)
    back = dot(total.astype(BF), wr_ref[...]).astype(BF)
    out_ref[...] = dot(back, wg_ref[...]).astype(BF)


def part_body(
    back_ref, links_hbm, latent_hbm, ws_hbm, wo_hbm,
    out_ref, far_ref, wo_ref, own_ref, latent_ref, ws_ref, sem,
):
    copies = [(latent_hbm, latent_ref), (ws_hbm, ws_ref), (links_hbm.at[0], own_ref)]
    copies += [(links_hbm.at[1:3], far_ref), (wo_hbm, wo_ref)]
    copies = start_all(copies, sem)
    copies[0].wait()
    copies[1].wait()
    total = dot(latent_ref[...], ws_ref[...])
    copies[2].wait()
    out_ref[...] = total + dot(own_ref[...], back_ref[...])
    copies[3].wait()
    copies[4].wait()


def final_body(part_ref, links_ref, near_ref, cross_ref, wo_ref, out_ref):
    total = part_ref[...] + dot(links_ref[0], near_ref[...])
    total = total + dot(links_ref[1], cross_ref[...])
    out_ref[...] = dot_nt(wo_ref[...], silu(total).astype(BF)).astype(BF)


def shards(
    grid_in,
    mesh_embed,
    g2m_src,
    g2m_dst,
    g2m_own_src,
    g2m_own_dst,
    g2m_len,
    mesh_nbr,
    halo_rows,
    m2g_src,
    m2g_dst,
    m2g_own_src,
    m2g_own_dst,
    m2g_len,
    w_embed,
    w_send,
    w_mesh,
    attn_gain,
    w_query,
    w_key,
    w_value,
    w_project,
    mlp_gain,
    w_up,
    w_down,
    w_return,
    w_grid,
    w_skip,
    w_out,
):
    x = grid_in[0]
    rows, channels = x.shape
    mesh_rows, width = mesh_embed.shape
    bands = lax.axis_size("space")
    slots = g2m_src.shape[2]
    part = w_query.shape[0]
    piece = part // 2
    hidden = w_up.shape[1]
    published = halo_rows.shape[1]
    table = mesh_rows + bands * published
    g2m_count = g2m_len.reshape(-1)
    m2g_count = m2g_len.reshape(-1)
    w_deep = w_down.reshape(-1, piece, width)
    deep = w_deep.shape[0] // 4
    blocks = hidden // width
    square = (w_query, w_key, w_value, w_project)
    bind = functools.partial
    swap = [(i, i ^ 1) for i in range(bands)]
    chain = [(i, j) for i in range(bands) for j in (i - 1 + i % 2 * 2,) if 0 <= j < bands]

    def turn(block, d):
        return lax.ppermute(block, "member", [(i, i ^ d) for i in range(4)])

    def pass_on(block, route):
        return lax.ppermute(block, "space", route)

    def like(a):
        return "v", a.shape, a.dtype

    def tag(where, *arrays):
        return [(where, a) for a in arrays]

    near, cross, own_a, own_b, x, w_embed, g2m_own_src, g2m_own_dst = call(
        bind(pick_body, bands),
        [
            ("v", (slots + 16, channels), BF),
            ("v", (slots + 16, channels), BF),
            ("v", (4 + deep, piece, width), BF),
            ("v", (deep + blocks, piece, width), BF),
            *map(like, (x, w_embed, g2m_own_src, g2m_own_dst)),
        ],
        tag("h", x, g2m_src[0], m2g_src[0], *square, w_up, w_deep, w_embed, g2m_own_src)
        + tag("h", g2m_own_dst),
        [
            pltpu.VMEM(g2m_src.shape[1:], jnp.int32),
            pltpu.VMEM(m2g_src.shape[1:], jnp.int32),
            pltpu.SemaphoreType.DMA((20,)),
        ],
        flops=int(3e8),
        nbytes=int(3e6),
    )
    a1 = turn(own_a, 1)
    b3 = turn(own_b, 3)
    near = pass_on(near, swap)
    cross = pass_on(cross, chain)
    b1 = turn(own_b, 1)
    a3 = turn(own_a, 3)
    a2 = turn(a1, 3)
    b2 = turn(b3, 1)
    ahead = [
        g2m_dst[0],
        w_send,
        w_mesh,
        mesh_embed,
        attn_gain.reshape(1, width),
        m2g_own_src,
        m2g_own_dst,
        m2g_dst[0],
        mesh_nbr.T,
    ]
    latent, agg, *ahead = call(
        bind(embed_body, len(ahead)),
        [("h", (rows, width), BF), ("v", (mesh_rows, width), F32), *map(like, ahead)],
        tag("v", x, w_embed, g2m_own_src, g2m_own_dst) + tag("s", g2m_count) + tag("h", *ahead),
        [pltpu.VMEM((rows, width), BF), pltpu.SemaphoreType.DMA((len(ahead) + 1,))],
        flops=int(3e9),
        nbytes=int(3e6),
    )
    state, normed, halo = call(
        bind(mesh_body, bands),
        [
            ("v", (mesh_rows, width), BF),
            ("v", (mesh_rows, width), BF),
            ("d", (bands * published, width), BF),
        ],
        tag("v", agg)
        + tag("d", near, cross)
        + tag("v", ahead[0])
        + tag("s", g2m_count)
        + tag("v", w_embed, *ahead[1:5])
        + tag("s", halo_rows),
        [pltpu.VMEM((mesh_rows, width), F32), pltpu.VMEM((published, width), F32)],
        flops=int(1e9),
        nbytes=int(3e6),
    )
    far = lax.all_to_all(halo, "space", 0, 0, tiled=True)
    links, repeats = call(
        bind(fill_body, bands),
        [("h", (3, rows, mesh_rows), BF), ("v", (mesh_rows, table), F32)],
        tag("v", *ahead[5:8])
        + tag("s", m2g_count)
        + tag("d", near, cross)
        + tag("v", ahead[8]),
        [pltpu.VMEM((3, rows, mesh_rows), BF), pltpu.SemaphoreType.DMA((1,))],
        flops=int(4e9),
        nbytes=int(8e6),
    )
    fetched = a1, b1, a3, b3, a2, b2
    shared = [pass_on(w, swap) for w in fetched]
    (back,) = call(
        layer_body,
        [("v", (mesh_rows, width), BF)],
        tag("v", normed)
        + tag("d", far)
        + tag("v", repeats, state)
        + tag("h", mlp_gain.reshape(1, width), w_return, w_grid)
        + tag("h", *square, w_up, w_deep, *fetched, *shared),
        [
            pltpu.VMEM((4, 4 * part, width), BF),
            pltpu.VMEM((blocks, 4 * part, width), BF),
            pltpu.VMEM((16 * deep, piece, width), BF),
            pltpu.VMEM((mesh_rows, width), BF),
            pltpu.VMEM((1, width), F32),
            pltpu.VMEM((width, width), BF),
            pltpu.VMEM((width, width), BF),
            pltpu.SemaphoreType.DMA((64,)),
        ],
        flops=int(5e9),
        nbytes=int(6e6),
    )
    back_near = pass_on(back, swap)
    back_cross = pass_on(back, chain)
    part, far_links, w_last = call(
        part_body,
        [("v", (rows, width), F32), ("v", (2, rows, mesh_rows), BF), like(w_out.T)],
        tag("v", back) + tag("h", links, latent, w_skip, w_out.T),
        [
            pltpu.VMEM((rows, mesh_rows), BF),
            pltpu.VMEM((rows, width), BF),
            pltpu.VMEM((width, width), BF),
            pltpu.SemaphoreType.DMA((5,)),
        ],
        flops=int(1e9),
        nbytes=int(2e6),
    )
    (result,) = call(
        final_body,
        [("d", (w_out.shape[1], rows), BF)],
        tag("v", part, far_links) + tag("d", back_near, back_cross) + tag("v", w_last),
        flops=int(2e9),
        nbytes=int(8e6),
    )
    return result[None]


def solution(mesh):
    placed = (
        P("member", "space", None),
        P("space", None),
        P("space", None, None),
        P("space", None, None),
        P("space", None),
        P("space", None),
        P(None, "space"),
        P("space", None),
        P("space", None),
        P("space", None, None),
        P("space", None, None),
        P("space", None),
        P("space", None),
        P(None, "space"),
        P(),
        P(),
        P(),
        P(),
        P("member", None),
        P("member", None),
        P("member", None),
        P("member", None),
        P(),
        P("member", None),
        P("member", None),
        P(),
        P(),
        P(),
        P(),
    )
    return jax.shard_map(
        shards, mesh=mesh, in_specs=placed, out_specs=P("member", None, "space"), check_vma=False
    )
```

```python
import functools
import math

import jax
import jax.numpy as jnp
from jax import lax
from jax.experimental import pallas as pl
from jax.experimental.pallas import tpu as pltpu
from jax.sharding import PartitionSpec as P

DH = 128
EPS = 1e-05
LOG2E = math.log2(math.e)
BF = jnp.bfloat16
F32 = jnp.float32

ANY = pl.BlockSpec(memory_space=pl.ANY)
HBM = pl.BlockSpec(memory_space=pltpu.HBM)
VMEM = pl.BlockSpec(memory_space=pltpu.VMEM)
SMEM = pl.BlockSpec(memory_space=pltpu.SMEM)


def dot(a, b):
    return jnp.dot(a, b, preferred_element_type=F32)


def dot_nt(a, b):
    return lax.dot_general(a, b, (((1,), (1,)), ((), ())), preferred_element_type=F32)


def silu(v):
    half = 0.5 * v
    return half + half * jnp.tanh(half)


def hot_rows(row, count):
    ids = lax.broadcasted_iota(jnp.int32, (count, row.shape[1]), 0)
    return jnp.where(ids == row, 1.0, 0.0).astype(BF)


def live(row, length):
    slot = lax.broadcasted_iota(jnp.int32, row.shape, 1)
    return jnp.where(slot < length, row, -1)


def layer_norm(values, gain):
    centred = values - jnp.mean(values, axis=-1, keepdims=True)
    spread = jnp.mean(centred * centred, axis=-1, keepdims=True)
    return centred * lax.rsqrt(spread + EPS) * gain


def call(body, outs, operands, scratch=(), flops=0, nbytes=0, mib=24):
    specs = {"h": HBM, "v": VMEM, "d": VMEM, "s": SMEM, "a": ANY}
    spaces = {"h": pltpu.HBM, "v": pltpu.VMEM}
    arrays = [
        pltpu.with_memory_space_constraint(a, spaces[w]) if w in spaces else a for w, a in operands
    ]
    kinds = {"h": pltpu.HBM, "v": pltpu.VMEM, "d": jax.ShapeDtypeStruct}
    shapes = [kinds[w](s, d) for w, s, d in outs]
    return pl.pallas_call(
        body,
        out_shape=shapes,
        in_specs=[specs[w] for w, _ in operands],
        out_specs=[specs[w] for w, _, _ in outs],
        scratch_shapes=list(scratch),
        compiler_params=pltpu.CompilerParams(vmem_limit_bytes=mib * 2**20),
        cost_estimate=pl.CostEstimate(flops=flops, bytes_accessed=nbytes, transcendentals=0),
    )(*arrays)


def around(bands):
    band = lax.axis_index("space")
    odd = band % 2
    cross = band - 1 + 2 * odd
    there = (cross >= 0) & (cross < bands)
    return band, band + 1 - 2 * odd, jnp.clip(cross, 0, bands - 1), there


def pick_body(
    bands, x_hbm, src_hbm, back_hbm, wq, wk, wv, wp, wu, wd, we_hbm, own_hbm, land_hbm,
    near_ref, cross_ref, a_ref, b_ref, x_ref, we_ref, own_ref, land_ref, src_ref, back_ref, sem,
):
    band, near, cross, _ = around(bands)
    copies = [(src_hbm, src_ref), (back_hbm, back_ref), (x_hbm, x_ref)]
    copies += half_weights((wq, wk, wv, wp), wu, wd, band % 2, a_ref, b_ref)
    copies += [(we_hbm, we_ref), (own_hbm, own_ref), (land_hbm, land_ref)]
    copies = start_all(copies, sem)
    for copy in copies[:3]:
        copy.wait()
    x = x_ref[...]
    rows = x.shape[0]
    slots = src_ref.shape[1]
    eye = lax.broadcasted_iota(jnp.int32, (slots, slots), 0) == lax.broadcasted_iota(
        jnp.int32, (slots, slots), 1
    )
    for out, at in ((near_ref, near), (cross_ref, cross)):
        wanted = src_ref[pl.ds(at, 1), :].astype(F32)
        column = jnp.sum(jnp.where(eye, wanted, 0.0), axis=1, keepdims=True).astype(jnp.int32)
        ids = lax.broadcasted_iota(jnp.int32, (slots, rows), 1)
        picker = jnp.where(ids == column, 1.0, 0.0).astype(BF)
        out[0:slots, :] = dot(picker, x).astype(BF)
        back = back_ref[pl.ds(at, 1), :].astype(F32)
        out[slots:, :] = jnp.broadcast_to(back, (out.shape[0] - slots, slots)).astype(BF)
    for copy in copies[3:]:
        copy.wait()


def start_all(pairs, sem, first=0):
    copies = [pltpu.make_async_copy(s, d, sem.at[first + i]) for i, (s, d) in enumerate(pairs)]
    for copy in copies:
        copy.start()
    return copies


def half_weights(square, wu, wd, half, a_ref, b_ref):
    _, piece, width = a_ref.shape
    top = pl.multiple_of(half * piece, piece)
    deep = wd.shape[0] // 4
    low = half * 2 * deep
    count = len(square)
    pairs = [(w.at[pl.ds(top, piece)], a_ref.at[i]) for i, w in enumerate(square)]
    pairs.append((wd.at[pl.ds(low, deep)], a_ref.at[count:]))
    pairs.append((wd.at[pl.ds(low + deep, deep)], b_ref.at[0:deep]))
    for i in range(wu.shape[1] // width):
        pairs.append(
            (wu.at[pl.ds(top, piece), i * width : (i + 1) * width], b_ref.at[deep + i])
        )
    return pairs


def embed_body(count, x_ref, we_ref, src_ref, dst_ref, len_ref, *refs):
    far, (latent_hbm, agg_ref), near, (latent_ref, sem) = (
        refs[:count],
        refs[count : count + 2],
        refs[count + 2 : -2],
        refs[-2:],
    )
    copies = start_all(list(zip(far, near)), sem)
    band = lax.axis_index("space")
    latent = silu(dot(x_ref[...], we_ref[...])).astype(BF)
    latent_ref[...] = latent
    copies += start_all([(latent_ref, latent_hbm)], sem, count)
    mesh_rows = agg_ref.shape[0]
    src_hot = hot_rows(src_ref[...], x_ref.shape[0])
    dst_hot = hot_rows(live(dst_ref[...], len_ref[band]), mesh_rows)
    links = dot_nt(dst_hot, src_hot).astype(BF)
    agg_ref[...] = dot(links, latent)
    for copy in copies:
        copy.wait()


def mesh_body(
    bands,
    agg_ref,
    near_ref,
    cross_ref,
    dst_ref,
    len_ref,
    we_ref,
    ws_ref,
    wm_ref,
    static_ref,
    gain_ref,
    rows_ref,
    state_ref,
    normed_ref,
    halo_ref,
    wide,
    own,
):
    _, near, cross, there = around(bands)
    total = agg_ref[...]
    mesh_rows = total.shape[0]
    slots = dst_ref.shape[1]
    for ref, at, some in ((near_ref, near, True), (cross_ref, cross, there)):
        count = jnp.where(some, len_ref[at], 0)
        latent = silu(dot(ref[0:slots, :], we_ref[...])).astype(BF)
        dst_hot = hot_rows(live(dst_ref[pl.ds(at, 1), :], count), mesh_rows)
        total = total + dot(dst_hot, latent)
    agg = dot(total.astype(BF), ws_ref[...]).astype(BF)
    state = (static_ref[...].astype(F32) + silu(dot(agg, wm_ref[...]))).astype(BF)
    state_ref[...] = state
    normed = layer_norm(state.astype(F32), gain_ref[...]).astype(BF)
    normed_ref[...] = normed
    wide[...] = normed.astype(F32)
    published = own.shape[0]
    for j in range(published):
        own[j : j + 1, :] = wide[pl.ds(rows_ref[0, j], 1), :]
    halo = own[...].astype(BF)
    for b in range(bands):
        halo_ref[b * published : (b + 1) * published, :] = halo


def fill_body(
    bands, src_ref, dst_ref, far_dst_ref, len_ref, near_ref, cross_ref, nbr_ref,
    links_hbm, rep_ref, links_ref, sem,
):
    band, near, cross, there = around(bands)
    mesh_rows, table = rep_ref.shape
    rows = links_ref.shape[1]
    slots = far_dst_ref.shape[1]
    src_hot = hot_rows(src_ref[...], mesh_rows)
    dst_hot = hot_rows(live(dst_ref[...], len_ref[band]), rows)
    links_ref[0] = dot_nt(dst_hot, src_hot).astype(BF)
    for i, (ref, at, some) in enumerate(((near_ref, near, True), (cross_ref, cross, there))):
        count = jnp.where(some, len_ref[at], 0)
        src = ref[slots : slots + 1, :].astype(F32).astype(jnp.int32)
        src_hot = hot_rows(src, mesh_rows)
        dst_hot = hot_rows(live(far_dst_ref[pl.ds(at, 1), :], count), rows)
        links_ref[i + 1] = dot_nt(dst_hot, src_hot).astype(BF)
    copies = start_all([(links_ref, links_hbm)], sem)
    labels = jnp.transpose(nbr_ref[...], (1, 0))
    ids = lax.broadcasted_iota(jnp.int32, (mesh_rows, table), 1)
    own = lax.broadcasted_iota(jnp.int32, (mesh_rows, 1), 0)
    repeats = jnp.where(ids == own, 1.0, 0.0)
    for k in range(labels.shape[1]):
        repeats = repeats + jnp.where(ids == labels[:, k : k + 1], 1.0, 0.0)
    rep_ref[...] = repeats.astype(BF)
    for copy in copies:
        copy.wait()


def layer_body(
    normed_ref, far_ref, rep_ref, state_ref, gain_hbm, wr_hbm, wg_hbm, wq, wk, wv, wp, wu, wd, *refs
):
    pieces, refs = refs[:12], refs[12:]
    out_ref, m_ref, u_ref, d_ref, att_ref, bias_ref, gain_ref, wr_ref, wg_ref, sem = refs
    me = lax.axis_index("member")
    half = lax.axis_index("space") % 2
    square = (wq, wk, wv, wp)
    count = len(square)
    part, width = wq.shape
    piece = part // 2
    deep = wd.shape[0] // 4
    blocks = wu.shape[1] // width
    home = pl.multiple_of(me * part, part)
    heads = [(w, m_ref.at[i, pl.ds(home, part)]) for i, w in enumerate(square)]
    ups = [
        (wu.at[:, i * width : (i + 1) * width], u_ref.at[i, pl.ds(home, part)])
        for i in range(blocks)
    ]
    downs = [(wd, d_ref.at[pl.ds(me * 4 * deep, 4 * deep)])]
    for j, d in enumerate((1, 3, 2)):
        source = me ^ d
        for side, (a, b) in ((half, pieces[2 * j : 2 * j + 2]), (1 - half, pieces[2 * j + 6 : 2 * j + 8])):
            at = pl.multiple_of(source * part + side * piece, piece)
            low = (source * 2 + side) * 2 * deep
            heads.append((a.at[0:count], m_ref.at[:, pl.ds(at, piece)]))
            ups.append((b.at[deep:], u_ref.at[:, pl.ds(at, piece)]))
            downs.append((a.at[count:], d_ref.at[pl.ds(low, deep)]))
            downs.append((b.at[0:deep], d_ref.at[pl.ds(low + deep, deep)]))
    heads = start_all(heads, sem)
    ups = start_all(ups, sem, len(heads))
    downs += [(wr_hbm, wr_ref), (wg_hbm, wg_ref)]
    heads_gain = start_all([(gain_hbm, gain_ref)], sem, len(heads) + len(ups) + len(downs))
    downs = start_all(downs, sem, len(heads) + len(ups))
    bias_ref[...] = jnp.log(rep_ref[...].astype(F32)) * LOG2E
    for copy in heads + heads_gain:
        copy.wait()
    normed = normed_ref[...]
    far = far_ref[...]
    queries = dot(normed, m_ref[0]).astype(BF)
    keys = jnp.concatenate([dot(normed, m_ref[1]).astype(BF), dot(far, m_ref[1]).astype(BF)], 0)
    values = jnp.concatenate([dot(normed, m_ref[2]).astype(BF), dot(far, m_ref[2]).astype(BF)], 0)
    for h in range(width // DH):
        at = slice(h * DH, (h + 1) * DH)
        scores = dot_nt(queries[:, at], keys[:, at]) * (LOG2E / math.sqrt(DH)) + bias_ref[...]
        weights = jnp.exp2(scores - jnp.max(scores, axis=-1, keepdims=True))
        total = jnp.sum(weights, axis=-1, keepdims=True)
        att_ref[:, at] = (dot(weights.astype(BF), values[:, at]) / total).astype(BF)
    after = state_ref[...].astype(F32) + dot(att_ref[...], m_ref[3])
    normed = layer_norm(after, gain_ref[...]).astype(BF)
    for copy in ups + downs:
        copy.wait()
    total = after
    span = width // piece
    for i in range(blocks):
        expanded = silu(dot(normed, u_ref[i])).astype(BF)
        down = d_ref[i * span : (i + 1) * span].reshape(width, width)
        total = total + dot(expanded, down)
    back = dot(total.astype(BF), wr_ref[...]).astype(BF)
    out_ref[...] = dot(back, wg_ref[...]).astype(BF)


def part_body(
    back_ref, links_hbm, latent_hbm, ws_hbm, wo_hbm,
    out_ref, far_ref, wo_ref, own_ref, latent_ref, ws_ref, sem,
):
    copies = [(latent_hbm, latent_ref), (ws_hbm, ws_ref), (links_hbm.at[0], own_ref)]
    copies += [(links_hbm.at[1:3], far_ref), (wo_hbm, wo_ref)]
    copies = start_all(copies, sem)
    copies[0].wait()
    copies[1].wait()
    total = dot(latent_ref[...], ws_ref[...])
    copies[2].wait()
    out_ref[...] = total + dot(own_ref[...], back_ref[...])
    copies[3].wait()
    copies[4].wait()


def final_body(part_ref, links_ref, near_ref, cross_ref, wo_ref, out_ref):
    total = part_ref[...] + dot(links_ref[0], near_ref[...])
    total = total + dot(links_ref[1], cross_ref[...])
    out_ref[...] = dot_nt(wo_ref[...], silu(total).astype(BF)).astype(BF)


def shards(
    grid_in,
    mesh_embed,
    g2m_src,
    g2m_dst,
    g2m_own_src,
    g2m_own_dst,
    g2m_len,
    mesh_nbr,
    halo_rows,
    m2g_src,
    m2g_dst,
    m2g_own_src,
    m2g_own_dst,
    m2g_len,
    w_embed,
    w_send,
    w_mesh,
    attn_gain,
    w_query,
    w_key,
    w_value,
    w_project,
    mlp_gain,
    w_up,
    w_down,
    w_return,
    w_grid,
    w_skip,
    w_out,
):
    x = grid_in[0]
    rows, channels = x.shape
    mesh_rows, width = mesh_embed.shape
    bands = lax.axis_size("space")
    slots = g2m_src.shape[2]
    part = w_query.shape[0]
    piece = part // 2
    hidden = w_up.shape[1]
    published = halo_rows.shape[1]
    table = mesh_rows + bands * published
    g2m_count = g2m_len.reshape(-1)
    m2g_count = m2g_len.reshape(-1)
    w_deep = w_down.reshape(-1, piece, width)
    deep = w_deep.shape[0] // 4
    blocks = hidden // width
    square = (w_query, w_key, w_value, w_project)
    bind = functools.partial
    swap = [(i, i ^ 1) for i in range(bands)]
    chain = []
    for m in range(4):
        for i in range(bands):
            j = i - 1 + i % 2 * 2
            chain.append((m * bands + i, m * bands + j if 0 <= j < bands else (m ^ 1) * bands + i))

    def turn(block, d):
        return lax.ppermute(block, "member", [(i, i ^ d) for i in range(4)])

    def pass_on(block, route):
        axes = "space" if len(route) == bands else ("member", "space")
        return lax.ppermute(block, axes, route)

    def like(a):
        return "v", a.shape, a.dtype

    def tag(where, *arrays):
        return [(where, a) for a in arrays]

    near, cross, own_a, own_b, x, w_embed, g2m_own_src, g2m_own_dst = call(
        bind(pick_body, bands),
        [
            ("v", (slots + 16, channels), BF),
            ("v", (slots + 16, channels), BF),
            ("v", (4 + deep, piece, width), BF),
            ("v", (deep + blocks, piece, width), BF),
            *map(like, (x, w_embed, g2m_own_src, g2m_own_dst)),
        ],
        tag("h", x, g2m_src[0], m2g_src[0], *square, w_up, w_deep, w_embed, g2m_own_src)
        + tag("h", g2m_own_dst),
        [
            pltpu.VMEM(g2m_src.shape[1:], jnp.int32),
            pltpu.VMEM(m2g_src.shape[1:], jnp.int32),
            pltpu.SemaphoreType.DMA((20,)),
        ],
        flops=int(3e8),
        nbytes=int(3e6),
    )
    a1 = turn(own_a, 1)
    b3 = turn(own_b, 3)
    near = pass_on(near, swap)
    cross = pass_on(cross, chain)
    b1 = turn(own_b, 1)
    a3 = turn(own_a, 3)
    a2 = turn(a1, 3)
    b2 = turn(b3, 1)
    ahead = [
        g2m_dst[0],
        w_send,
        w_mesh,
        mesh_embed,
        attn_gain.reshape(1, width),
        m2g_own_src,
        m2g_own_dst,
        m2g_dst[0],
        mesh_nbr.T,
    ]
    latent, agg, *ahead = call(
        bind(embed_body, len(ahead)),
        [("h", (rows, width), BF), ("v", (mesh_rows, width), F32), *map(like, ahead)],
        tag("v", x, w_embed, g2m_own_src, g2m_own_dst) + tag("s", g2m_count) + tag("h", *ahead),
        [pltpu.VMEM((rows, width), BF), pltpu.SemaphoreType.DMA((len(ahead) + 1,))],
        flops=int(3e9),
        nbytes=int(3e6),
    )
    state, normed, halo = call(
        bind(mesh_body, bands),
        [
            ("v", (mesh_rows, width), BF),
            ("v", (mesh_rows, width), BF),
            ("v", (bands * published, width), BF),
        ],
        tag("v", agg)
        + tag("d", near, cross)
        + tag("v", ahead[0])
        + tag("s", g2m_count)
        + tag("v", w_embed, *ahead[1:5])
        + tag("s", halo_rows),
        [pltpu.VMEM((mesh_rows, width), F32), pltpu.VMEM((published, width), F32)],
        flops=int(1e9),
        nbytes=int(3e6),
    )
    far = lax.all_to_all(halo, "space", 0, 0, tiled=True)
    links, repeats = call(
        bind(fill_body, bands),
        [("h", (3, rows, mesh_rows), BF), ("v", (mesh_rows, table), BF)],
        tag("v", *ahead[5:8])
        + tag("s", m2g_count)
        + tag("d", near, cross)
        + tag("v", ahead[8]),
        [pltpu.VMEM((3, rows, mesh_rows), BF), pltpu.SemaphoreType.DMA((1,))],
        flops=int(4e9),
        nbytes=int(8e6),
    )
    fetched = a1, b1, a3, b3, a2, b2
    shared = [pass_on(w, swap) for w in fetched]
    (back,) = call(
        layer_body,
        [("v", (mesh_rows, width), BF)],
        tag("v", normed)
        + tag("d", far)
        + tag("v", repeats, state)
        + tag("h", mlp_gain.reshape(1, width), w_return, w_grid)
        + tag("h", *square, w_up, w_deep)
        + tag("h", *fetched)
        + [("v" if i in (0, 2, 3) else "h", w) for i, w in enumerate(shared)],
        [
            pltpu.VMEM((4, 4 * part, width), BF),
            pltpu.VMEM((blocks, 4 * part, width), BF),
            pltpu.VMEM((16 * deep, piece, width), BF),
            pltpu.VMEM((mesh_rows, width), BF),
            pltpu.VMEM((mesh_rows, table), F32),
            pltpu.VMEM((1, width), F32),
            pltpu.VMEM((width, width), BF),
            pltpu.VMEM((width, width), BF),
            pltpu.SemaphoreType.DMA((64,)),
        ],
        flops=int(5e9),
        nbytes=int(6e6),
    )
    back_near = pass_on(back, swap)
    back_cross = pass_on(back, chain)
    part, far_links, w_last = call(
        part_body,
        [("v", (rows, width), F32), ("v", (2, rows, mesh_rows), BF), like(w_out.T)],
        tag("v", back) + tag("h", links, latent, w_skip, w_out.T),
        [
            pltpu.VMEM((rows, mesh_rows), BF),
            pltpu.VMEM((rows, width), BF),
            pltpu.VMEM((width, width), BF),
            pltpu.SemaphoreType.DMA((5,)),
        ],
        flops=int(1e9),
        nbytes=int(2e6),
    )
    (result,) = call(
        final_body,
        [("d", (w_out.shape[1], rows), BF)],
        tag("v", part, far_links) + tag("d", back_near, back_cross) + tag("v", w_last),
        flops=int(2e9),
        nbytes=int(8e6),
    )
    return result[None]


def solution(mesh):
    placed = (
        P("member", "space", None),
        P("space", None),
        P("space", None, None),
        P("space", None, None),
        P("space", None),
        P("space", None),
        P(None, "space"),
        P("space", None),
        P("space", None),
        P("space", None, None),
        P("space", None, None),
        P("space", None),
        P("space", None),
        P(None, "space"),
        P(),
        P(),
        P(),
        P(),
        P("member", None),
        P("member", None),
        P("member", None),
        P("member", None),
        P(),
        P("member", None),
        P("member", None),
        P(),
        P(),
        P(),
        P(),
    )
    return jax.shard_map(
        shards, mesh=mesh, in_specs=placed, out_specs=P("member", None, "space"), check_vma=False
    )
```

```python
import functools
import math

import jax
import jax.numpy as jnp
from jax import lax
from jax.experimental import pallas as pl
from jax.experimental.pallas import tpu as pltpu
from jax.sharding import PartitionSpec as P

DH = 128
EPS = 1e-05
LOG2E = math.log2(math.e)
BF = jnp.bfloat16
F32 = jnp.float32

ANY = pl.BlockSpec(memory_space=pl.ANY)
HBM = pl.BlockSpec(memory_space=pltpu.HBM)
VMEM = pl.BlockSpec(memory_space=pltpu.VMEM)
SMEM = pl.BlockSpec(memory_space=pltpu.SMEM)


def dot(a, b):
    return jnp.dot(a, b, preferred_element_type=F32)


def dot_nt(a, b):
    return lax.dot_general(a, b, (((1,), (1,)), ((), ())), preferred_element_type=F32)


def silu(v):
    half = 0.5 * v
    return half + half * jnp.tanh(half)


def hot_rows(row, count):
    ids = lax.broadcasted_iota(jnp.int32, (count, row.shape[1]), 0)
    return jnp.where(ids == row, 1.0, 0.0).astype(BF)


def live(row, length):
    slot = lax.broadcasted_iota(jnp.int32, row.shape, 1)
    return jnp.where(slot < length, row, -1)


def length_at(len_ref, at, some=True):
    lanes = lax.broadcasted_iota(jnp.int32, len_ref.shape, 1)
    here = jnp.where((lanes == at) & some, len_ref[...].astype(F32), 0.0)
    return jnp.sum(here, axis=1, keepdims=True).astype(jnp.int32)


def layer_norm(values, gain):
    centred = values - jnp.mean(values, axis=-1, keepdims=True)
    spread = jnp.mean(centred * centred, axis=-1, keepdims=True)
    return centred * lax.rsqrt(spread + EPS) * gain


def call(body, outs, operands, scratch=(), flops=0, nbytes=0, mib=24):
    specs = {"h": HBM, "v": VMEM, "d": VMEM, "s": SMEM, "a": ANY}
    spaces = {"h": pltpu.HBM, "v": pltpu.VMEM}
    arrays = [
        pltpu.with_memory_space_constraint(a, spaces[w]) if w in spaces else a for w, a in operands
    ]
    kinds = {"h": pltpu.HBM, "v": pltpu.VMEM, "d": jax.ShapeDtypeStruct}
    shapes = [kinds[w](s, d) for w, s, d in outs]
    return pl.pallas_call(
        body,
        out_shape=shapes,
        in_specs=[specs[w] for w, _ in operands],
        out_specs=[specs[w] for w, _, _ in outs],
        scratch_shapes=list(scratch),
        compiler_params=pltpu.CompilerParams(vmem_limit_bytes=mib * 2**20),
        cost_estimate=pl.CostEstimate(flops=flops, bytes_accessed=nbytes, transcendentals=0),
    )(*arrays)


def around(bands):
    band = lax.axis_index("space")
    odd = band % 2
    cross = band - 1 + 2 * odd
    there = (cross >= 0) & (cross < bands)
    return band, band + 1 - 2 * odd, jnp.clip(cross, 0, bands - 1), there


def pick_body(
    bands, x_hbm, src_hbm, back_hbm, wq, wk, wv, wp, wu, wd, we_hbm, own_hbm, land_hbm,
    len_hbm, near_ref, cross_ref, a_ref, b_ref, x_ref, we_ref, own_ref, land_ref, len_ref,
    src_ref, back_ref, sem,
):
    band, near, cross, _ = around(bands)
    copies = [(src_hbm, src_ref), (back_hbm, back_ref), (x_hbm, x_ref)]
    copies += half_weights((wq, wk, wv, wp), wu, wd, band % 2, a_ref, b_ref)
    copies += [(we_hbm, we_ref), (own_hbm, own_ref), (land_hbm, land_ref), (len_hbm, len_ref)]
    copies = start_all(copies, sem)
    for copy in copies[:3]:
        copy.wait()
    x = x_ref[...]
    rows = x.shape[0]
    slots = src_ref.shape[1]
    eye = lax.broadcasted_iota(jnp.int32, (slots, slots), 0) == lax.broadcasted_iota(
        jnp.int32, (slots, slots), 1
    )
    for out, at in ((near_ref, near), (cross_ref, cross)):
        wanted = src_ref[pl.ds(at, 1), :].astype(F32)
        column = jnp.sum(jnp.where(eye, wanted, 0.0), axis=1, keepdims=True).astype(jnp.int32)
        ids = lax.broadcasted_iota(jnp.int32, (slots, rows), 1)
        picker = jnp.where(ids == column, 1.0, 0.0).astype(BF)
        out[0:slots, :] = dot(picker, x).astype(BF)
        back = back_ref[pl.ds(at, 1), :].astype(F32)
        out[slots:, :] = jnp.broadcast_to(back, (out.shape[0] - slots, slots)).astype(BF)
    for copy in copies[3:]:
        copy.wait()


def start_all(pairs, sem, first=0):
    copies = [pltpu.make_async_copy(s, d, sem.at[first + i]) for i, (s, d) in enumerate(pairs)]
    for copy in copies:
        copy.start()
    return copies


def half_weights(square, wu, wd, half, a_ref, b_ref):
    _, piece, width = a_ref.shape
    top = pl.multiple_of(half * piece, piece)
    deep = wd.shape[0] // 4
    low = half * 2 * deep
    count = len(square)
    pairs = [(w.at[pl.ds(top, piece)], a_ref.at[i]) for i, w in enumerate(square)]
    pairs.append((wd.at[pl.ds(low, deep)], a_ref.at[count:]))
    pairs.append((wd.at[pl.ds(low + deep, deep)], b_ref.at[0:deep]))
    for i in range(wu.shape[1] // width):
        pairs.append(
            (wu.at[pl.ds(top, piece), i * width : (i + 1) * width], b_ref.at[deep + i])
        )
    return pairs


def embed_body(count, x_ref, we_ref, src_ref, dst_ref, len_ref, *refs):
    far, (latent_hbm, agg_ref), near, (latent_ref, sem) = (
        refs[:count],
        refs[count : count + 2],
        refs[count + 2 : -2],
        refs[-2:],
    )
    copies = start_all(list(zip(far, near)), sem)
    band = lax.axis_index("space")
    latent = silu(dot(x_ref[...], we_ref[...])).astype(BF)
    latent_ref[...] = latent
    copies += start_all([(latent_ref, latent_hbm)], sem, count)
    mesh_rows = agg_ref.shape[0]
    src_hot = hot_rows(src_ref[...], x_ref.shape[0])
    dst_hot = hot_rows(live(dst_ref[...], length_at(len_ref, band)), mesh_rows)
    links = dot_nt(dst_hot, src_hot).astype(BF)
    agg_ref[...] = dot(links, latent)
    for copy in copies:
        copy.wait()


def mesh_body(
    bands,
    agg_ref,
    near_ref,
    cross_ref,
    dst_ref,
    len_ref,
    we_ref,
    ws_ref,
    wm_ref,
    static_ref,
    gain_ref,
    rows_ref,
    state_ref,
    normed_ref,
    halo_ref,
):
    _, near, cross, there = around(bands)
    total = agg_ref[...]
    mesh_rows = total.shape[0]
    slots = dst_ref.shape[1]
    for ref, at, some in ((near_ref, near, True), (cross_ref, cross, there)):
        count = length_at(len_ref, at, some)
        latent = silu(dot(ref[0:slots, :], we_ref[...])).astype(BF)
        dst_hot = hot_rows(live(dst_ref[pl.ds(at, 1), :], count), mesh_rows)
        total = total + dot(dst_hot, latent)
    agg = dot(total.astype(BF), ws_ref[...]).astype(BF)
    state = (static_ref[...].astype(F32) + silu(dot(agg, wm_ref[...]))).astype(BF)
    state_ref[...] = state
    normed = layer_norm(state.astype(F32), gain_ref[...]).astype(BF)
    normed_ref[...] = normed
    published = rows_ref.shape[1]
    eye = lax.broadcasted_iota(jnp.int32, (published, published), 0) == lax.broadcasted_iota(
        jnp.int32, (published, published), 1
    )
    column = jnp.sum(jnp.where(eye, rows_ref[...].astype(F32), 0.0), axis=1, keepdims=True)
    ids = lax.broadcasted_iota(jnp.int32, (published, mesh_rows), 1)
    picker = jnp.where(ids == column.astype(jnp.int32), 1.0, 0.0).astype(BF)
    own = dot(picker, normed).astype(BF)
    split = own.shape[1] // 2
    halves = own[:, :split], own[:, split:]
    for b in range(bands):
        halo_ref[b * published : (b + 1) * published, :] = halves[b % 2]


def count_labels(nbr_ref, lab_ref, inc_ref, acc_ref, rep_ref):
    mesh_rows, table = rep_ref.shape
    fields = table // mesh_rows
    labels = nbr_ref[...]
    local, step = labels, jnp.ones_like(labels)
    for f in range(1, fields):
        local = jnp.where(labels >= f * mesh_rows, labels - f * mesh_rows, local)
        step = jnp.where(labels >= f * mesh_rows, 1 << (10 * f), step)
    lab_ref[...] = local
    inc_ref[...] = step
    chunk = 64
    for c in range(0, mesh_rows, chunk):
        ids = lax.broadcasted_iota(jnp.int32, (chunk, mesh_rows), 0) + c
        total = jnp.where(ids == lax.broadcasted_iota(jnp.int32, ids.shape, 1), 1, 0)
        for k in range(labels.shape[0]):
            total = total + jnp.where(ids == lab_ref[k : k + 1, :], inc_ref[k : k + 1, :], 0)
        acc_ref[c : c + chunk, :] = total
    counts = jnp.transpose(acc_ref[...], (1, 0))
    for f in range(fields):
        part = (counts >> (10 * f)) & 1023
        rep_ref[:, f * mesh_rows : (f + 1) * mesh_rows] = part.astype(F32).astype(BF)


def fill_body(
    bands, src_ref, dst_ref, far_dst_ref, len_ref, near_ref, cross_ref, nbr_ref,
    links_hbm, rep_ref, links_ref, lab_ref, inc_ref, acc_ref, sem,
):
    band, near, cross, there = around(bands)
    mesh_rows, _ = rep_ref.shape
    rows = links_ref.shape[1]
    slots = far_dst_ref.shape[1]
    src_hot = hot_rows(src_ref[...], mesh_rows)
    dst_hot = hot_rows(live(dst_ref[...], length_at(len_ref, band)), rows)
    links_ref[0] = dot_nt(dst_hot, src_hot).astype(BF)
    for i, (ref, at, some) in enumerate(((near_ref, near, True), (cross_ref, cross, there))):
        count = length_at(len_ref, at, some)
        src = ref[slots : slots + 1, :].astype(F32).astype(jnp.int32)
        src_hot = hot_rows(src, mesh_rows)
        dst_hot = hot_rows(live(far_dst_ref[pl.ds(at, 1), :], count), rows)
        links_ref[i + 1] = dot_nt(dst_hot, src_hot).astype(BF)
    copies = start_all([(links_ref, links_hbm)], sem)
    count_labels(nbr_ref, lab_ref, inc_ref, acc_ref, rep_ref)
    for copy in copies:
        copy.wait()


def layer_body(
    normed_ref, far_ref, got_ref, rep_ref, state_ref, gain_hbm, wr_hbm, wg_hbm, wq, wk, wv, wp, wu, wd, *refs
):
    pieces, refs = refs[:12], refs[12:]
    out_ref, m_ref, u_ref, d_ref, att_ref, bias_ref, gain_ref, wr_ref, wg_ref, sem = refs
    me = lax.axis_index("member")
    half = lax.axis_index("space") % 2
    square = (wq, wk, wv, wp)
    count = len(square)
    part, width = wq.shape
    piece = part // 2
    deep = wd.shape[0] // 4
    blocks = wu.shape[1] // width
    home = pl.multiple_of(me * part, part)
    heads = [(w, m_ref.at[i, pl.ds(home, part)]) for i, w in enumerate(square)]
    ups = [
        (wu.at[:, i * width : (i + 1) * width], u_ref.at[i, pl.ds(home, part)])
        for i in range(blocks)
    ]
    downs = [(wd, d_ref.at[pl.ds(me * 4 * deep, 4 * deep)])]
    for j, d in enumerate((1, 3, 2)):
        source = me ^ d
        for side, (a, b) in ((half, pieces[2 * j : 2 * j + 2]), (1 - half, pieces[2 * j + 6 : 2 * j + 8])):
            at = pl.multiple_of(source * part + side * piece, piece)
            low = (source * 2 + side) * 2 * deep
            heads.append((a.at[0:count], m_ref.at[:, pl.ds(at, piece)]))
            ups.append((b.at[deep:], u_ref.at[:, pl.ds(at, piece)]))
            downs.append((a.at[count:], d_ref.at[pl.ds(low, deep)]))
            downs.append((b.at[0:deep], d_ref.at[pl.ds(low + deep, deep)]))
    heads = start_all(heads, sem)
    ups = start_all(ups, sem, len(heads))
    downs += [(wr_hbm, wr_ref), (wg_hbm, wg_ref)]
    heads_gain = start_all([(gain_hbm, gain_ref)], sem, len(heads) + len(ups) + len(downs))
    downs = start_all(downs, sem, len(heads) + len(ups))
    bias_ref[...] = jnp.log(rep_ref[...].astype(F32)) * LOG2E
    for copy in heads + heads_gain:
        copy.wait()
    normed = normed_ref[...]
    mine, other = far_ref[...], got_ref[...]
    first = half == 0
    far = jnp.concatenate([jnp.where(first, mine, other), jnp.where(first, other, mine)], 1)
    queries = dot(normed, m_ref[0]).astype(BF)
    keys = jnp.concatenate([dot(normed, m_ref[1]).astype(BF), dot(far, m_ref[1]).astype(BF)], 0)
    values = jnp.concatenate([dot(normed, m_ref[2]).astype(BF), dot(far, m_ref[2]).astype(BF)], 0)
    for h in range(width // DH):
        at = slice(h * DH, (h + 1) * DH)
        scores = dot_nt(queries[:, at], keys[:, at]) * (LOG2E / math.sqrt(DH)) + bias_ref[...]
        weights = jnp.exp2(scores - jnp.max(scores, axis=-1, keepdims=True))
        total = jnp.sum(weights, axis=-1, keepdims=True)
        att_ref[:, at] = (dot(weights.astype(BF), values[:, at]) / total).astype(BF)
    after = state_ref[...].astype(F32) + dot(att_ref[...], m_ref[3])
    normed = layer_norm(after, gain_ref[...]).astype(BF)
    for copy in ups + downs:
        copy.wait()
    total = after
    span = width // piece
    for i in range(blocks):
        expanded = silu(dot(normed, u_ref[i])).astype(BF)
        down = d_ref[i * span : (i + 1) * span].reshape(width, width)
        total = total + dot(expanded, down)
    back = dot(total.astype(BF), wr_ref[...]).astype(BF)
    out_ref[...] = dot(back, wg_ref[...]).astype(BF)


def part_body(
    back_ref, near_ref, links_hbm, latent_hbm, ws_hbm, wo_hbm,
    out_ref, far_ref, wo_ref, own_ref, latent_ref, ws_ref, sem,
):
    copies = [(latent_hbm, latent_ref), (ws_hbm, ws_ref), (links_hbm.at[0:2], own_ref)]
    copies += [(links_hbm.at[2], far_ref), (wo_hbm, wo_ref)]
    copies = start_all(copies, sem)
    copies[0].wait()
    copies[1].wait()
    total = dot(latent_ref[...], ws_ref[...])
    copies[2].wait()
    total = total + dot(own_ref[0], back_ref[...])
    out_ref[...] = total + dot(own_ref[1], near_ref[...])
    copies[3].wait()
    copies[4].wait()


def final_body(part_ref, links_ref, cross_ref, wo_ref, out_ref):
    total = part_ref[...] + dot(links_ref[...], cross_ref[...])
    out_ref[...] = dot_nt(wo_ref[...], silu(total).astype(BF)).astype(BF)


def shards(
    grid_in,
    mesh_embed,
    g2m_src,
    g2m_dst,
    g2m_own_src,
    g2m_own_dst,
    g2m_len,
    mesh_nbr,
    halo_rows,
    m2g_src,
    m2g_dst,
    m2g_own_src,
    m2g_own_dst,
    m2g_len,
    w_embed,
    w_send,
    w_mesh,
    attn_gain,
    w_query,
    w_key,
    w_value,
    w_project,
    mlp_gain,
    w_up,
    w_down,
    w_return,
    w_grid,
    w_skip,
    w_out,
):
    x = grid_in[0]
    rows, channels = x.shape
    mesh_rows, width = mesh_embed.shape
    bands = lax.axis_size("space")
    slots = g2m_src.shape[2]
    part = w_query.shape[0]
    piece = part // 2
    hidden = w_up.shape[1]
    published = halo_rows.shape[1]
    table = mesh_rows + bands * published
    g2m_count = g2m_len.reshape(1, -1)
    m2g_count = m2g_len.reshape(1, -1)
    w_deep = w_down.reshape(-1, piece, width)
    deep = w_deep.shape[0] // 4
    blocks = hidden // width
    square = (w_query, w_key, w_value, w_project)
    bind = functools.partial
    swap = [(i, i ^ 1) for i in range(bands)]
    chain = []
    for m in range(4):
        for i in range(bands):
            j = i - 1 + i % 2 * 2
            chain.append((m * bands + i, m * bands + j if 0 <= j < bands else (m ^ 1) * bands + i))

    def turn(block, d):
        return lax.ppermute(block, "member", [(i, i ^ d) for i in range(4)])

    def pass_on(block, route):
        axes = "space" if len(route) == bands else ("member", "space")
        return lax.ppermute(block, axes, route)

    def like(a):
        return "v", a.shape, a.dtype

    def tag(where, *arrays):
        return [(where, a) for a in arrays]

    near, cross, own_a, own_b, x, w_embed, g2m_own_src, g2m_own_dst, g2m_count = call(
        bind(pick_body, bands),
        [
            ("v", (slots + 16, channels), BF),
            ("v", (slots + 16, channels), BF),
            ("v", (4 + deep, piece, width), BF),
            ("v", (deep + blocks, piece, width), BF),
            *map(like, (x, w_embed, g2m_own_src, g2m_own_dst, g2m_count)),
        ],
        tag("h", x, g2m_src[0], m2g_src[0], *square, w_up, w_deep, w_embed, g2m_own_src)
        + tag("h", g2m_own_dst, g2m_count),
        [
            pltpu.VMEM(g2m_src.shape[1:], jnp.int32),
            pltpu.VMEM(m2g_src.shape[1:], jnp.int32),
            pltpu.SemaphoreType.DMA((20,)),
        ],
        flops=int(3e8),
        nbytes=int(3e6),
    )
    a1 = turn(own_a, 1)
    b3 = turn(own_b, 3)
    near = pass_on(near, swap)
    cross = pass_on(cross, chain)
    b1 = turn(own_b, 1)
    a3 = turn(own_a, 3)
    a2 = turn(a1, 3)
    b2 = turn(b3, 1)
    ahead = [
        g2m_dst[0],
        w_send,
        w_mesh,
        mesh_embed,
        attn_gain.reshape(1, width),
        m2g_own_src,
        m2g_own_dst,
        m2g_dst[0],
        mesh_nbr.T,
        halo_rows,
        m2g_count,
    ]
    latent, agg, *ahead = call(
        bind(embed_body, len(ahead)),
        [("h", (rows, width), BF), ("v", (mesh_rows, width), F32), *map(like, ahead)],
        tag("v", x, w_embed, g2m_own_src, g2m_own_dst, g2m_count) + tag("h", *ahead),
        [pltpu.VMEM((rows, width), BF), pltpu.SemaphoreType.DMA((len(ahead) + 1,))],
        flops=int(3e9),
        nbytes=int(3e6),
    )
    state, normed, halo = call(
        bind(mesh_body, bands),
        [
            ("v", (mesh_rows, width), BF),
            ("v", (mesh_rows, width), BF),
            ("v", (bands * published, width // 2), BF),
        ],
        tag("v", agg)
        + tag("d", near, cross)
        + tag("v", ahead[0])
        + tag("v", g2m_count, w_embed, *ahead[1:5], ahead[9]),
        flops=int(1e9),
        nbytes=int(3e6),
    )
    far = lax.all_to_all(halo, "space", 0, 0, tiled=True)
    got = pass_on(far, swap)
    links, repeats = call(
        bind(fill_body, bands),
        [("h", (3, rows, mesh_rows), BF), ("v", (mesh_rows, table), BF)],
        tag("v", *ahead[5:8])
        + tag("v", ahead[10])
        + tag("d", near, cross)
        + tag("v", ahead[8]),
        [
            pltpu.VMEM((3, rows, mesh_rows), BF),
            pltpu.VMEM(ahead[8].shape, jnp.int32),
            pltpu.VMEM(ahead[8].shape, jnp.int32),
            pltpu.VMEM((mesh_rows, mesh_rows), jnp.int32),
            pltpu.SemaphoreType.DMA((1,)),
        ],
        flops=int(4e9),
        nbytes=int(8e6),
    )
    fetched = a1, b1, a3, b3, a2, b2
    shared = [pass_on(w, swap) for w in fetched]
    (back,) = call(
        layer_body,
        [("v", (mesh_rows, width), BF)],
        tag("v", normed)
        + tag("d", far, got)
        + tag("v", repeats, state)
        + tag("h", mlp_gain.reshape(1, width), w_return, w_grid)
        + tag("h", *square, w_up, w_deep)
        + tag("h", *fetched)
        + [("v" if i in (4, 5) else "h", w) for i, w in enumerate(shared)],
        [
            pltpu.VMEM((4, 4 * part, width), BF),
            pltpu.VMEM((blocks, 4 * part, width), BF),
            pltpu.VMEM((16 * deep, piece, width), BF),
            pltpu.VMEM((mesh_rows, width), BF),
            pltpu.VMEM((mesh_rows, table), F32),
            pltpu.VMEM((1, width), F32),
            pltpu.VMEM((width, width), BF),
            pltpu.VMEM((width, width), BF),
            pltpu.SemaphoreType.DMA((64,)),
        ],
        flops=int(5e9),
        nbytes=int(6e6),
    )
    back_near = pass_on(back, swap)
    back_cross = pass_on(back, chain)
    part, far_links, w_last = call(
        part_body,
        [("v", (rows, width), F32), ("v", (rows, mesh_rows), BF), like(w_out.T)],
        tag("v", back) + tag("d", back_near) + tag("h", links, latent, w_skip, w_out.T),
        [
            pltpu.VMEM((2, rows, mesh_rows), BF),
            pltpu.VMEM((rows, width), BF),
            pltpu.VMEM((width, width), BF),
            pltpu.SemaphoreType.DMA((5,)),
        ],
        flops=int(1e9),
        nbytes=int(2e6),
    )
    (result,) = call(
        final_body,
        [("d", (w_out.shape[1], rows), BF)],
        tag("v", part, far_links) + tag("d", back_cross) + tag("v", w_last),
        flops=int(2e9),
        nbytes=int(8e6),
    )
    return result[None]


def solution(mesh):
    placed = (
        P("member", "space", None),
        P("space", None),
        P("space", None, None),
        P("space", None, None),
        P("space", None),
        P("space", None),
        P(None, "space"),
        P("space", None),
        P("space", None),
        P("space", None, None),
        P("space", None, None),
        P("space", None),
        P("space", None),
        P(None, "space"),
        P(),
        P(),
        P(),
        P(),
        P("member", None),
        P("member", None),
        P("member", None),
        P("member", None),
        P(),
        P("member", None),
        P("member", None),
        P(),
        P(),
        P(),
        P(),
    )
    return jax.shard_map(
        shards, mesh=mesh, in_specs=placed, out_specs=P("member", None, "space"), check_vma=False
    )
```

```python
import functools
import math

import jax
import jax.numpy as jnp
from jax import lax
from jax.experimental import pallas as pl
from jax.experimental.pallas import tpu as pltpu
from jax.sharding import PartitionSpec as P

DH = 128
EPS = 1e-05
LOG2E = math.log2(math.e)
BF = jnp.bfloat16
F32 = jnp.float32

ANY = pl.BlockSpec(memory_space=pl.ANY)
HBM = pl.BlockSpec(memory_space=pltpu.HBM)
VMEM = pl.BlockSpec(memory_space=pltpu.VMEM)
SMEM = pl.BlockSpec(memory_space=pltpu.SMEM)


def dot(a, b):
    return jnp.dot(a, b, preferred_element_type=F32)


def dot_nt(a, b):
    return lax.dot_general(a, b, (((1,), (1,)), ((), ())), preferred_element_type=F32)


def silu(v):
    half = 0.5 * v
    return half + half * jnp.tanh(half)


def hot_rows(row, count):
    ids = lax.broadcasted_iota(jnp.int32, (count, row.shape[1]), 0)
    return jnp.where(ids == row, 1.0, 0.0).astype(BF)


def live(row, length):
    slot = lax.broadcasted_iota(jnp.int32, row.shape, 1)
    return jnp.where(slot < length, row, -1)


def length_at(len_ref, at, some=True):
    lanes = lax.broadcasted_iota(jnp.int32, len_ref.shape, 1)
    here = jnp.where((lanes == at) & some, len_ref[...].astype(F32), 0.0)
    return jnp.sum(here, axis=1, keepdims=True).astype(jnp.int32)


def layer_norm(values, gain):
    centred = values - jnp.mean(values, axis=-1, keepdims=True)
    spread = jnp.mean(centred * centred, axis=-1, keepdims=True)
    return centred * lax.rsqrt(spread + EPS) * gain


def call(body, outs, operands, scratch=(), flops=0, nbytes=0, mib=24):
    specs = {"h": HBM, "v": VMEM, "d": VMEM, "s": SMEM, "a": ANY}
    spaces = {"h": pltpu.HBM, "v": pltpu.VMEM}
    arrays = [
        pltpu.with_memory_space_constraint(a, spaces[w]) if w in spaces else a for w, a in operands
    ]
    kinds = {"h": pltpu.HBM, "v": pltpu.VMEM, "d": jax.ShapeDtypeStruct}
    shapes = [kinds[w](s, d) for w, s, d in outs]
    return pl.pallas_call(
        body,
        out_shape=shapes,
        in_specs=[specs[w] for w, _ in operands],
        out_specs=[specs[w] for w, _, _ in outs],
        scratch_shapes=list(scratch),
        compiler_params=pltpu.CompilerParams(vmem_limit_bytes=mib * 2**20),
        cost_estimate=pl.CostEstimate(flops=flops, bytes_accessed=nbytes, transcendentals=0),
    )(*arrays)


def around(bands):
    band = lax.axis_index("space")
    odd = band % 2
    cross = band - 1 + 2 * odd
    there = (cross >= 0) & (cross < bands)
    return band, band + 1 - 2 * odd, jnp.clip(cross, 0, bands - 1), there


def pick_body(
    bands, x_hbm, src_hbm, back_hbm, wq, wk, wv, wp, wu, wd, we_hbm, own_hbm, land_hbm,
    len_hbm, near_ref, cross_ref, a_ref, b_ref, x_ref, we_ref, own_ref, land_ref, len_ref,
    src_ref, back_ref, sem,
):
    band, near, cross, _ = around(bands)
    copies = [(src_hbm, src_ref), (back_hbm, back_ref), (x_hbm, x_ref)]
    copies += half_weights((wq, wk, wv, wp), wu, wd, band % 2, a_ref, b_ref)
    copies += [(we_hbm, we_ref), (own_hbm, own_ref), (land_hbm, land_ref), (len_hbm, len_ref)]
    copies = start_all(copies, sem)
    for copy in copies[:3]:
        copy.wait()
    x = x_ref[...]
    rows = x.shape[0]
    slots = src_ref.shape[1]
    eye = lax.broadcasted_iota(jnp.int32, (slots, slots), 0) == lax.broadcasted_iota(
        jnp.int32, (slots, slots), 1
    )
    for out, at in ((near_ref, near), (cross_ref, cross)):
        wanted = src_ref[pl.ds(at, 1), :].astype(F32)
        column = jnp.sum(jnp.where(eye, wanted, 0.0), axis=1, keepdims=True).astype(jnp.int32)
        ids = lax.broadcasted_iota(jnp.int32, (slots, rows), 1)
        picker = jnp.where(ids == column, 1.0, 0.0).astype(BF)
        out[0:slots, :] = dot(picker, x).astype(BF)
        back = back_ref[pl.ds(at, 1), :].astype(F32)
        out[slots:, :] = jnp.broadcast_to(back, (out.shape[0] - slots, slots)).astype(BF)
    for copy in copies[3:]:
        copy.wait()


def start_all(pairs, sem, first=0):
    copies = [pltpu.make_async_copy(s, d, sem.at[first + i]) for i, (s, d) in enumerate(pairs)]
    for copy in copies:
        copy.start()
    return copies


def half_weights(square, wu, wd, half, a_ref, b_ref):
    _, piece, width = a_ref.shape
    top = pl.multiple_of(half * piece, piece)
    deep = wd.shape[0] // 4
    low = half * 2 * deep
    count = len(square)
    pairs = [(w.at[pl.ds(top, piece)], a_ref.at[i]) for i, w in enumerate(square)]
    pairs.append((wd.at[pl.ds(low, deep)], a_ref.at[count:]))
    pairs.append((wd.at[pl.ds(low + deep, deep)], b_ref.at[0:deep]))
    for i in range(wu.shape[1] // width):
        pairs.append(
            (wu.at[pl.ds(top, piece), i * width : (i + 1) * width], b_ref.at[deep + i])
        )
    return pairs


def embed_body(count, x_ref, we_ref, src_ref, dst_ref, len_ref, *refs):
    far, (latent_hbm, agg_ref), near, (latent_ref, sem) = (
        refs[:count],
        refs[count : count + 2],
        refs[count + 2 : -2],
        refs[-2:],
    )
    copies = start_all(list(zip(far, near)), sem)
    band = lax.axis_index("space")
    latent = silu(dot(x_ref[...], we_ref[...])).astype(BF)
    latent_ref[...] = latent
    copies += start_all([(latent_ref, latent_hbm)], sem, count)
    mesh_rows = agg_ref.shape[0]
    src_hot = hot_rows(src_ref[...], x_ref.shape[0])
    dst_hot = hot_rows(live(dst_ref[...], length_at(len_ref, band)), mesh_rows)
    links = dot_nt(dst_hot, src_hot).astype(BF)
    agg_ref[...] = dot(links, latent)
    for copy in copies:
        copy.wait()


def mesh_body(
    bands,
    agg_ref,
    near_ref,
    cross_ref,
    dst_ref,
    len_ref,
    we_ref,
    ws_ref,
    wm_ref,
    static_ref,
    gain_ref,
    rows_ref,
    state_ref,
    normed_ref,
    halo_ref,
):
    _, near, cross, there = around(bands)
    total = agg_ref[...]
    mesh_rows = total.shape[0]
    slots = dst_ref.shape[1]
    for ref, at, some in ((near_ref, near, True), (cross_ref, cross, there)):
        count = length_at(len_ref, at, some)
        latent = silu(dot(ref[0:slots, :], we_ref[...])).astype(BF)
        dst_hot = hot_rows(live(dst_ref[pl.ds(at, 1), :], count), mesh_rows)
        total = total + dot(dst_hot, latent)
    agg = dot(total.astype(BF), ws_ref[...]).astype(BF)
    state = (static_ref[...].astype(F32) + silu(dot(agg, wm_ref[...]))).astype(BF)
    state_ref[...] = state
    normed = layer_norm(state.astype(F32), gain_ref[...]).astype(BF)
    normed_ref[...] = normed
    published = rows_ref.shape[1]
    eye = lax.broadcasted_iota(jnp.int32, (published, published), 0) == lax.broadcasted_iota(
        jnp.int32, (published, published), 1
    )
    column = jnp.sum(jnp.where(eye, rows_ref[...].astype(F32), 0.0), axis=1, keepdims=True)
    ids = lax.broadcasted_iota(jnp.int32, (published, mesh_rows), 1)
    picker = jnp.where(ids == column.astype(jnp.int32), 1.0, 0.0).astype(BF)
    own = dot(picker, normed).astype(BF)
    split = own.shape[1] // 2
    halves = own[:, :split], own[:, split:]
    for b in range(bands):
        halo_ref[b * published : (b + 1) * published, :] = halves[b % 2]


def count_labels(nbr_ref, lab_ref, inc_ref, acc_ref, rep_ref):
    mesh_rows, table = rep_ref.shape
    fields = table // mesh_rows
    labels = nbr_ref[...]
    local, step = labels, jnp.ones_like(labels)
    for f in range(1, fields):
        local = jnp.where(labels >= f * mesh_rows, labels - f * mesh_rows, local)
        step = jnp.where(labels >= f * mesh_rows, 1 << (10 * f), step)
    lab_ref[...] = local
    inc_ref[...] = step
    chunk = 64
    for c in range(0, mesh_rows, chunk):
        ids = lax.broadcasted_iota(jnp.int32, (chunk, mesh_rows), 0) + c
        total = jnp.where(ids == lax.broadcasted_iota(jnp.int32, ids.shape, 1), 1, 0)
        for k in range(labels.shape[0]):
            total = total + jnp.where(ids == lab_ref[k : k + 1, :], inc_ref[k : k + 1, :], 0)
        acc_ref[c : c + chunk, :] = total
    counts = jnp.transpose(acc_ref[...], (1, 0))
    for f in range(fields):
        part = (counts >> (10 * f)) & 1023
        rep_ref[:, f * mesh_rows : (f + 1) * mesh_rows] = part.astype(F32).astype(BF)


def fill_body(
    bands, src_ref, dst_ref, far_dst_ref, len_ref, near_ref, cross_ref, nbr_ref,
    links_hbm, rep_ref, links_ref, lab_ref, inc_ref, acc_ref, sem,
):
    band, near, cross, there = around(bands)
    mesh_rows, _ = rep_ref.shape
    rows = links_ref.shape[1]
    slots = far_dst_ref.shape[1]
    src_hot = hot_rows(src_ref[...], mesh_rows)
    dst_hot = hot_rows(live(dst_ref[...], length_at(len_ref, band)), rows)
    links_ref[0] = dot_nt(dst_hot, src_hot).astype(BF)
    for i, (ref, at, some) in enumerate(((near_ref, near, True), (cross_ref, cross, there))):
        count = length_at(len_ref, at, some)
        src = ref[slots : slots + 1, :].astype(F32).astype(jnp.int32)
        src_hot = hot_rows(src, mesh_rows)
        dst_hot = hot_rows(live(far_dst_ref[pl.ds(at, 1), :], count), rows)
        links_ref[i + 1] = dot_nt(dst_hot, src_hot).astype(BF)
    copies = start_all([(links_ref, links_hbm)], sem)
    count_labels(nbr_ref, lab_ref, inc_ref, acc_ref, rep_ref)
    for copy in copies:
        copy.wait()


def layer_body(
    normed_ref, far_ref, got_ref, rep_ref, state_ref, gain_hbm, wr_hbm, wg_hbm, wq, wk, wv, wp, wu, wd, *refs
):
    pieces, refs = refs[:12], refs[12:]
    out_ref, m_ref, u_ref, d_ref, att_ref, bias_ref, gain_ref, wr_ref, wg_ref, sem = refs
    me = lax.axis_index("member")
    half = lax.axis_index("space") % 2
    square = (wq, wk, wv, wp)
    count = len(square)
    part, width = wq.shape
    piece = part // 2
    deep = wd.shape[0] // 4
    blocks = wu.shape[1] // width
    home = pl.multiple_of(me * part, part)
    heads = [(w, m_ref.at[i, pl.ds(home, part)]) for i, w in enumerate(square)]
    ups = [
        (wu.at[:, i * width : (i + 1) * width], u_ref.at[i, pl.ds(home, part)])
        for i in range(blocks)
    ]
    downs = [(wd, d_ref.at[pl.ds(me * 4 * deep, 4 * deep)])]
    for j, d in enumerate((1, 3, 2)):
        source = me ^ d
        for side, (a, b) in ((half, pieces[2 * j : 2 * j + 2]), (1 - half, pieces[2 * j + 6 : 2 * j + 8])):
            at = pl.multiple_of(source * part + side * piece, piece)
            low = (source * 2 + side) * 2 * deep
            heads.append((a.at[0:count], m_ref.at[:, pl.ds(at, piece)]))
            ups.append((b.at[deep:], u_ref.at[:, pl.ds(at, piece)]))
            downs.append((a.at[count:], d_ref.at[pl.ds(low, deep)]))
            downs.append((b.at[0:deep], d_ref.at[pl.ds(low + deep, deep)]))
    heads = start_all(heads, sem)
    downs += [(gain_hbm, gain_ref), (wr_hbm, wr_ref), (wg_hbm, wg_ref)]
    bias_ref[...] = jnp.log(rep_ref[...].astype(F32)) * LOG2E
    for copy in heads:
        copy.wait()
    ups = start_all(ups, sem, len(heads))
    downs = start_all(downs, sem, len(heads) + len(ups))
    normed = normed_ref[...]
    mine, other = far_ref[...], got_ref[...]
    first = half == 0
    far = jnp.concatenate([jnp.where(first, mine, other), jnp.where(first, other, mine)], 1)
    queries = dot(normed, m_ref[0]).astype(BF)
    keys = jnp.concatenate([dot(normed, m_ref[1]).astype(BF), dot(far, m_ref[1]).astype(BF)], 0)
    values = jnp.concatenate([dot(normed, m_ref[2]).astype(BF), dot(far, m_ref[2]).astype(BF)], 0)
    ones = jnp.ones((values.shape[0], DH), BF)
    for h in range(width // DH):
        at = slice(h * DH, (h + 1) * DH)
        scores = dot_nt(queries[:, at], keys[:, at]) * (LOG2E / math.sqrt(DH)) + bias_ref[...]
        weights = jnp.exp2(scores - jnp.max(scores, axis=-1, keepdims=True))
        both = jnp.concatenate([values[:, at], ones], 1)
        mixed = dot(weights.astype(BF), both)
        att_ref[:, at] = (mixed[:, :DH] / mixed[:, DH:]).astype(BF)
    after = state_ref[...].astype(F32) + dot(att_ref[...], m_ref[3])
    for copy in ups + downs:
        copy.wait()
    normed = layer_norm(after, gain_ref[...]).astype(BF)
    total = after
    span = width // piece
    for i in range(blocks):
        expanded = silu(dot(normed, u_ref[i])).astype(BF)
        down = d_ref[i * span : (i + 1) * span].reshape(width, width)
        total = total + dot(expanded, down)
    back = dot(total.astype(BF), wr_ref[...]).astype(BF)
    out_ref[...] = dot(back, wg_ref[...]).astype(BF)


def part_body(
    back_ref, near_ref, links_hbm, latent_hbm, ws_hbm, wo_hbm,
    out_ref, far_ref, wo_ref, own_ref, latent_ref, ws_ref, sem,
):
    copies = [(latent_hbm, latent_ref), (ws_hbm, ws_ref), (links_hbm.at[0:2], own_ref)]
    copies += [(links_hbm.at[2], far_ref), (wo_hbm, wo_ref)]
    copies = start_all(copies, sem)
    copies[0].wait()
    copies[1].wait()
    total = dot(latent_ref[...], ws_ref[...])
    copies[2].wait()
    total = total + dot(own_ref[0], back_ref[...])
    out_ref[...] = total + dot(own_ref[1], near_ref[...])
    copies[3].wait()
    copies[4].wait()


def final_body(part_ref, links_ref, cross_ref, wo_ref, out_ref):
    total = part_ref[...] + dot(links_ref[...], cross_ref[...])
    out_ref[...] = dot_nt(wo_ref[...], silu(total).astype(BF)).astype(BF)


def shards(
    grid_in,
    mesh_embed,
    g2m_src,
    g2m_dst,
    g2m_own_src,
    g2m_own_dst,
    g2m_len,
    mesh_nbr,
    halo_rows,
    m2g_src,
    m2g_dst,
    m2g_own_src,
    m2g_own_dst,
    m2g_len,
    w_embed,
    w_send,
    w_mesh,
    attn_gain,
    w_query,
    w_key,
    w_value,
    w_project,
    mlp_gain,
    w_up,
    w_down,
    w_return,
    w_grid,
    w_skip,
    w_out,
):
    x = grid_in[0]
    rows, channels = x.shape
    mesh_rows, width = mesh_embed.shape
    bands = lax.axis_size("space")
    slots = g2m_src.shape[2]
    part = w_query.shape[0]
    piece = part // 2
    hidden = w_up.shape[1]
    published = halo_rows.shape[1]
    table = mesh_rows + bands * published
    g2m_count = g2m_len.reshape(1, -1)
    m2g_count = m2g_len.reshape(1, -1)
    w_deep = w_down.reshape(-1, piece, width)
    deep = w_deep.shape[0] // 4
    blocks = hidden // width
    square = (w_query, w_key, w_value, w_project)
    bind = functools.partial
    swap = [(i, i ^ 1) for i in range(bands)]
    chain = []
    for m in range(4):
        for i in range(bands):
            j = i - 1 + i % 2 * 2
            chain.append((m * bands + i, m * bands + j if 0 <= j < bands else (m ^ 1) * bands + i))

    def turn(block, d):
        return lax.ppermute(block, "member", [(i, i ^ d) for i in range(4)])

    def pass_on(block, route):
        axes = "space" if len(route) == bands else ("member", "space")
        return lax.ppermute(block, axes, route)

    def like(a):
        return "v", a.shape, a.dtype

    def tag(where, *arrays):
        return [(where, a) for a in arrays]

    near, cross, own_a, own_b, x, w_embed, g2m_own_src, g2m_own_dst, g2m_count = call(
        bind(pick_body, bands),
        [
            ("v", (slots + 16, channels), BF),
            ("v", (slots + 16, channels), BF),
            ("v", (4 + deep, piece, width), BF),
            ("v", (deep + blocks, piece, width), BF),
            *map(like, (x, w_embed, g2m_own_src, g2m_own_dst, g2m_count)),
        ],
        tag("h", x, g2m_src[0], m2g_src[0], *square, w_up, w_deep, w_embed, g2m_own_src)
        + tag("h", g2m_own_dst, g2m_count),
        [
            pltpu.VMEM(g2m_src.shape[1:], jnp.int32),
            pltpu.VMEM(m2g_src.shape[1:], jnp.int32),
            pltpu.SemaphoreType.DMA((20,)),
        ],
        flops=int(3e8),
        nbytes=int(3e6),
    )
    a1 = turn(own_a, 1)
    b3 = turn(own_b, 3)
    near = pass_on(near, swap)
    cross = pass_on(cross, chain)
    b1 = turn(own_b, 1)
    a3 = turn(own_a, 3)
    a2 = turn(a1, 3)
    b2 = turn(b3, 1)
    ahead = [
        g2m_dst[0],
        w_send,
        w_mesh,
        mesh_embed,
        attn_gain.reshape(1, width),
        m2g_own_src,
        m2g_own_dst,
        m2g_dst[0],
        mesh_nbr.T,
        halo_rows,
        m2g_count,
    ]
    latent, agg, *ahead = call(
        bind(embed_body, len(ahead)),
        [("h", (rows, width), BF), ("v", (mesh_rows, width), F32), *map(like, ahead)],
        tag("v", x, w_embed, g2m_own_src, g2m_own_dst, g2m_count) + tag("h", *ahead),
        [pltpu.VMEM((rows, width), BF), pltpu.SemaphoreType.DMA((len(ahead) + 1,))],
        flops=int(3e9),
        nbytes=int(3e6),
    )
    state, normed, halo = call(
        bind(mesh_body, bands),
        [
            ("v", (mesh_rows, width), BF),
            ("v", (mesh_rows, width), BF),
            ("v", (bands * published, width // 2), BF),
        ],
        tag("v", agg)
        + tag("d", near, cross)
        + tag("v", ahead[0])
        + tag("v", g2m_count, w_embed, *ahead[1:5], ahead[9]),
        flops=int(1e9),
        nbytes=int(3e6),
    )
    far = lax.all_to_all(halo, "space", 0, 0, tiled=True)
    got = pass_on(far, swap)
    links, repeats = call(
        bind(fill_body, bands),
        [("h", (3, rows, mesh_rows), BF), ("v", (mesh_rows, table), BF)],
        tag("v", *ahead[5:8])
        + tag("v", ahead[10])
        + tag("d", near, cross)
        + tag("v", ahead[8]),
        [
            pltpu.VMEM((3, rows, mesh_rows), BF),
            pltpu.VMEM(ahead[8].shape, jnp.int32),
            pltpu.VMEM(ahead[8].shape, jnp.int32),
            pltpu.VMEM((mesh_rows, mesh_rows), jnp.int32),
            pltpu.SemaphoreType.DMA((1,)),
        ],
        flops=int(4e9),
        nbytes=int(8e6),
    )
    fetched = a1, b1, a3, b3, a2, b2
    shared = [pass_on(w, swap) for w in fetched]
    (back,) = call(
        layer_body,
        [("v", (mesh_rows, width), BF)],
        tag("v", normed)
        + tag("d", far, got)
        + tag("v", repeats, state)
        + tag("h", mlp_gain.reshape(1, width), w_return, w_grid)
        + tag("h", *square, w_up, w_deep)
        + tag("h", *fetched)
        + [("v" if i in (4, 5) else "h", w) for i, w in enumerate(shared)],
        [
            pltpu.VMEM((4, 4 * part, width), BF),
            pltpu.VMEM((blocks, 4 * part, width), BF),
            pltpu.VMEM((16 * deep, piece, width), BF),
            pltpu.VMEM((mesh_rows, width), BF),
            pltpu.VMEM((mesh_rows, table), F32),
            pltpu.VMEM((1, width), F32),
            pltpu.VMEM((width, width), BF),
            pltpu.VMEM((width, width), BF),
            pltpu.SemaphoreType.DMA((64,)),
        ],
        flops=int(5e9),
        nbytes=int(6e6),
    )
    back_near = pass_on(back, swap)
    back_cross = pass_on(back, chain)
    part, far_links, w_last = call(
        part_body,
        [("v", (rows, width), F32), ("v", (rows, mesh_rows), BF), like(w_out.T)],
        tag("v", back) + tag("d", back_near) + tag("h", links, latent, w_skip, w_out.T),
        [
            pltpu.VMEM((2, rows, mesh_rows), BF),
            pltpu.VMEM((rows, width), BF),
            pltpu.VMEM((width, width), BF),
            pltpu.SemaphoreType.DMA((5,)),
        ],
        flops=int(1e9),
        nbytes=int(2e6),
    )
    (result,) = call(
        final_body,
        [("d", (w_out.shape[1], rows), BF)],
        tag("v", part, far_links) + tag("d", back_cross) + tag("v", w_last),
        flops=int(2e9),
        nbytes=int(8e6),
    )
    return result[None]


def solution(mesh):
    placed = (
        P("member", "space", None),
        P("space", None),
        P("space", None, None),
        P("space", None, None),
        P("space", None),
        P("space", None),
        P(None, "space"),
        P("space", None),
        P("space", None),
        P("space", None, None),
        P("space", None, None),
        P("space", None),
        P("space", None),
        P(None, "space"),
        P(),
        P(),
        P(),
        P(),
        P("member", None),
        P("member", None),
        P("member", None),
        P("member", None),
        P(),
        P("member", None),
        P("member", None),
        P(),
        P(),
        P(),
        P(),
    )
    return jax.shard_map(
        shards, mesh=mesh, in_specs=placed, out_specs=P("member", None, "space"), check_vma=False
    )
```
